32 devices in a mesh: dp: 8 (over y, x, core), tensor: 4 (over z).
Axes of the slice: x: 2, y: 2, z: 4, core: 2. Of those that a mesh axis runs over, the one named last changes fastest.
Arguments:
- tokens: bfloat16 [2, 8192, 2048], P(None, ('dp', 'tensor')), may hold values from -6 to 6
- segments: int32 [2, 8, 1024], P(None, 'dp'), may hold values from 0 to 15, never falling along the last dimension, each value on 1 to 512 neighbouring positions
- query_weight: bfloat16 [2048, 2048], P('dp', 'tensor'), may hold values from -0.125 to 0.125
- key_weight: bfloat16 [2048, 2048], P('dp', 'tensor'), may hold values from -0.125 to 0.125
- value_weight: bfloat16 [2048, 2048], P('dp', 'tensor'), may hold values from -0.125 to 0.125
- output_weight: bfloat16 [2048, 2048], P('tensor', 'dp'), may hold values from -0.75 to 0.75
- expand_weight: bfloat16 [2048, 8192], P('dp', 'tensor'), may hold values from -0.125 to 0.125
- contract_weight: bfloat16 [8192, 2048], P('tensor', 'dp'), may hold values from -0.09375 to 0.09375
- norm_gains: bfloat16 [2, 2048], P(None, 'dp'), may hold values from 0.099609375 to 1.8984375
- norm_shifts: bfloat16 [2, 2048], P(None, 'dp'), may hold values from -1.75 to 1.75
- cotangent: bfloat16 [2, 8192, 2048], P(None, ('dp', 'tensor')), may hold values from -6 to 6
Outputs:
- result: bfloat16 [2, 8192, 2048], P(None, ('dp', 'tensor'))
- tokens_grad: float32 [2, 8192, 2048], P(None, ('dp', 'tensor'))
- query_grad: float32 [2048, 2048], P('dp', 'tensor')
- key_grad: float32 [2048, 2048], P('dp', 'tensor')
- value_grad: float32 [2048, 2048], P('dp', 'tensor')
- output_grad: float32 [2048, 2048], P('tensor', 'dp')
- expand_grad: float32 [2048, 8192], P('dp', 'tensor')
- contract_grad: float32 [8192, 2048], P('tensor', 'dp')
- gains_grad: float32 [2, 2048], P(None, 'dp')
- shifts_grad: float32 [2, 2048], P(None, 'dp')
The draws below stay inside these ranges and needn't reach their ends.
Inputs may be any that keep to these rules, and one draw needn't show every extreme that they name: `segments`: along each packed row of 1024 tokens the numbers never fall; each document has 1 to 512 tokens. Numbers only compare tokens of the same row.
All inputs are finite; a program needn't handle non-finite values.
Results may differ from the reference program's by a relative error of at most 0.019.
Values may be sent and summed in bfloat16 or wider, within the bound.
No kernel may reach another device: no remote copies, remote signals or barrier semaphores. Data moves between devices by JAX's collectives and lax.ppermute only.
A program may use at most 256 MiB of HBM per device.

```python
import math
import jax
import jax.numpy as jnp
import numpy as np
from jax import lax

D = 2048
HEADS = 16
DH = 128
FF = 8192
SEQ = 1024
DOCS = 16
ROWS = 1
MICRO = 2
TOKENS_MB = 8192
N_DP = 8


def level_of(key, extent, pieces, low, top_value):
    def one(axis_at, shards_of):
        steps = jax.random.uniform(jax.random.fold_in(jax.random.fold_in(key, 6), axis_at), (shards_of,), jnp.float32, low / len(pieces), top_value / len(pieces))
        return jnp.repeat(jnp.exp(steps), extent[axis_at] // shards_of).reshape((-1,) + (1,) * (len(extent) - axis_at - 1))

    loudness = one(*pieces[0])
    for cut in pieces[1:]:
        loudness = loudness * one(*cut)
    return loudness


def split_up(count, total, limit, lean):
    loads = [(1 << 20) // math.isqrt(standing ** lean) + 1 for standing in range(2, count + 1)]
    surplus, counts = total - limit - (count - 1), [1] * (count - 1)
    while surplus > 0:
        candidates = [i for i in range(count - 1) if counts[i] < limit]
        whole, remaining = sum([loads[i] for i in candidates]), surplus
        for i in candidates:
            addition = min(limit - counts[i], max(1, remaining * loads[i] // whole), surplus)
            counts[i] = counts[i] + addition
            surplus = surplus - addition
    return np.array([limit] + counts)


def uneven(rng, count, total, limit, slope):
    if count == 2:
        one = jax.random.randint(rng, (), max(1, total - limit), min(limit, total - 1) + 1)
        return jnp.stack([one, total - one])
    tallies = jnp.asarray(split_up(count, total, limit, slope), jnp.int32)
    twos = (count - 1) // 2
    donor, taker = tallies[1:1 + 2 * twos:2], tallies[2:2 + 2 * twos:2]
    margin = jnp.minimum(donor - 1, limit - taker)
    passed = jax.random.randint(jax.random.fold_in(rng, 1), (twos,), 0, 1 << 20) % (margin + 1)
    tallies = tallies.at[1:1 + 2 * twos:2].set(donor - passed).at[2:2 + 2 * twos:2].set(taker + passed)
    return tallies[jax.random.permutation(jax.random.fold_in(rng, 2), count)]


def gaussian(rng, extent, deviation, reach, cuts=(), kind=jnp.bfloat16):
    loudness = level_of(rng, extent, cuts, -0.22, 0.18) if cuts else 1.0
    values = jax.random.normal(rng, extent, jnp.float32) * deviation * loudness
    return jnp.minimum(jnp.maximum(values, -reach), reach).astype(kind)


def setup_inputs(seed: int = 0) -> dict:
    streams_of = jax.random.split(jax.random.key(seed), 12)
    return {
        "tokens": gaussian(streams_of[0], (MICRO, TOKENS_MB, D), 1.0, 6.0, ((1, 32),)),
        "segments": jax.vmap(lambda own: jnp.searchsorted(jnp.cumsum(uneven(own, DOCS, SEQ, SEQ // 2, 2)), jnp.arange(SEQ), side="right"))(jax.random.split(streams_of[1], MICRO * (N_DP * ROWS))).reshape((MICRO, N_DP * ROWS, SEQ)).astype(jnp.int32),
        "query_weight": gaussian(streams_of[2], (D, D), D ** -0.5, 0.125, ((0, 8), (1, 4))),
        "key_weight": gaussian(streams_of[3], (D, D), D ** -0.5, 0.125, ((0, 8), (1, 4))),
        "value_weight": gaussian(streams_of[4], (D, D), D ** -0.5, 0.125, ((0, 8), (1, 4))),
        "output_weight": gaussian(streams_of[5], (D, D), (D // 32) ** -0.5, 0.75, ((0, 4), (1, 8))),
        "expand_weight": gaussian(streams_of[6], (D, FF), D ** -0.5, 0.125, ((0, 8), (1, 4))),
        "contract_weight": gaussian(streams_of[7], (FF, D), (FF // 2) ** -0.5, 0.09375, ((0, 4), (1, 8))),
        "norm_gains": jnp.clip(1.0 + 0.18 * jax.random.normal(streams_of[8], (2, D), jnp.float32), 0.099609375, 1.8984375).astype(jnp.bfloat16),
        "norm_shifts": gaussian(streams_of[9], (2, D), 0.3, 1.75, ((1, 8),)),
        "cotangent": gaussian(streams_of[10], (MICRO, TOKENS_MB, D), 1.0, 6.0, ((1, 32),)),
    }


EPSILON = 1e-06
NEGATIVE = -1e+30
HIGHEST = lax.Precision.HIGHEST

@jax.custom_vjp
def low(v):
    return lax.optimization_barrier(v.astype(jnp.bfloat16)).astype(jnp.float32)

@jax.custom_vjp
def low_back(v):
    return v

def low_keep(v):
    return (low(v), None)

def low_pass(kept, grad):
    return (grad,)

def back_keep(v):
    return (v, None)

def back_low(kept, grad):
    return (low(grad),)
low.defvjp(low_keep, low_pass)
low_back.defvjp(back_keep, back_low)

def matmul(left, right):
    return jnp.dot(left, right, precision=HIGHEST, preferred_element_type=jnp.float32)

def layer_norm(values, gain, shift):
    average = lax.optimization_barrier(jnp.mean(values, axis=-1, keepdims=True))
    centered = values - average
    variance = lax.optimization_barrier(jnp.mean(centered * centered, axis=-1, keepdims=True))
    return centered * lax.rsqrt(variance + EPSILON) * gain + shift

def forward(tokens, segment_row, query_weight, key_weight, value_weight, output_weight, expand_weight, contract_weight, norm_gains, norm_shifts):
    length = tokens.shape[0]
    query = low(low_back(matmul(tokens, query_weight))).reshape(length, HEADS, DH)
    keys = low(low_back(matmul(tokens, key_weight))).reshape(length, HEADS, DH)
    values = low(low_back(matmul(tokens, value_weight))).reshape(length, HEADS, DH)
    scores = low_back(jnp.einsum('qhd,khd->hqk', query, keys, precision=HIGHEST) * DH ** (-0.5))
    matching = segment_row[:, None] == segment_row[None, :]
    scores = jnp.where(matching[None], scores, NEGATIVE)
    row_top = lax.optimization_barrier(jnp.max(scores, axis=-1, keepdims=True))
    exponent = jnp.exp(scores - row_top)
    probs = exponent / lax.optimization_barrier(jnp.sum(exponent, axis=-1, keepdims=True))
    context = jnp.einsum('hqk,khd->qhd', low(probs), values, precision=HIGHEST)
    context = low(low_back(context)).reshape(length, HEADS * DH)
    attended = low_back(matmul(context, output_weight))
    normed = layer_norm(tokens + attended, norm_gains[0], norm_shifts[0])
    hidden = low_back(matmul(low(normed), expand_weight))
    active = low(jax.nn.gelu(hidden, approximate=True))
    branch = low_back(matmul(active, contract_weight))
    return layer_norm(normed + branch, norm_gains[1], norm_shifts[1])

def reference(tokens, segments, query_weight, key_weight, value_weight, output_weight, expand_weight, contract_weight, norm_gains, norm_shifts, cotangent):
    row_count = MICRO * N_DP * ROWS
    token_rows = tokens.astype(jnp.float32).reshape(row_count, SEQ, D)
    grad_rows = cotangent.astype(jnp.float32).reshape(row_count, SEQ, D)
    segment_rows = segments.reshape(row_count, SEQ)
    params = (query_weight.astype(jnp.float32), key_weight.astype(jnp.float32), value_weight.astype(jnp.float32), output_weight.astype(jnp.float32), expand_weight.astype(jnp.float32), contract_weight.astype(jnp.float32), norm_gains.astype(jnp.float32), norm_shifts.astype(jnp.float32))

    def one_row(totals, inputs):
        row_tokens, row_segments, row_grad = inputs

        def apply(row_input, first, second, third, fourth, fifth, sixth, seventh, eighth):
            return forward(row_input, row_segments, first, second, third, fourth, fifth, sixth, seventh, eighth)
        outcome, pull = jax.vjp(apply, row_tokens, *params)
        grads = pull(row_grad)
        totals = tuple((total + piece for total, piece in zip(totals, grads[1:])))
        return (totals, (outcome.astype(jnp.bfloat16), grads[0]))
    starting = tuple((jnp.zeros_like(param) for param in params))
    totals, (outputs, input_grads) = lax.scan(one_row, starting, (token_rows, segment_rows, grad_rows))
    result = outputs.reshape(MICRO, N_DP * ROWS * SEQ, D)
    tokens_grad = input_grads.reshape(MICRO, N_DP * ROWS * SEQ, D)
    return (result, tokens_grad, totals[0], totals[1], totals[2], totals[3], totals[4], totals[5], totals[6], totals[7])
```

```python
import functools

import jax
import jax.numpy as jnp
from jax import lax
from jax.experimental import pallas as pl
from jax.experimental.pallas import tpu as pltpu
from jax.sharding import PartitionSpec as P

DH = 128
EPSILON = 1e-06
NEGATIVE = -1e30
AXES = ("dp", "tensor")
F32 = jnp.float32
BF16 = jnp.bfloat16


def dot_nn(left, right):
    return jnp.dot(left, right, preferred_element_type=F32)


def dot_tn(left, right):
    return lax.dot_general(left, right, (((0,), (0,)), ((), ())), preferred_element_type=F32)


def dot_nt(left, right):
    return lax.dot_general(left, right, (((1,), (1,)), ((), ())), preferred_element_type=F32)


def attention_forward_kernel(qkv_ref, seg_col_ref, seg_row_ref, out_ref, *, block):
    length = qkv_ref.shape[0]
    keys = qkv_ref[:, DH : 2 * DH]
    values = qkv_ref[:, 2 * DH :]
    seg_row = seg_row_ref[...]
    for start in range(0, length, block):
        rows = slice(start, start + block)
        scores = dot_nt(qkv_ref[rows, :DH], keys)
        scores = jnp.where(seg_col_ref[rows, :] == seg_row, scores, NEGATIVE)
        top = jnp.max(scores, axis=1, keepdims=True)
        exponent = jnp.exp((scores - top) * DH**-0.5)
        total = jnp.sum(exponent, axis=1, keepdims=True)
        context = dot_nn(exponent.astype(BF16), values)
        out_ref[rows, :] = (context / total).astype(BF16)


def attention_backward_kernel(
    qkv_ref, grad_ref, seg_col_ref, seg_row_ref, out_ref, key_total, value_total, *, block
):
    length = qkv_ref.shape[0]
    keys = qkv_ref[:, DH : 2 * DH]
    values = qkv_ref[:, 2 * DH :]
    seg_col = seg_col_ref[...]
    for start in range(0, length, block):
        rows = slice(start, start + block)
        query = qkv_ref[rows, :DH]
        grad = grad_ref[rows, :]
        scores = dot_nt(keys, query)
        scores = jnp.where(seg_col == seg_row_ref[:, rows], scores, NEGATIVE)
        top = jnp.max(scores, axis=0, keepdims=True)
        exponent = jnp.exp((scores - top) * DH**-0.5)
        probs = exponent * (1.0 / jnp.sum(exponent, axis=0, keepdims=True))
        prob_grad = dot_nt(values, grad)
        weighted = jnp.sum(probs * prob_grad, axis=0, keepdims=True)
        score_grad = (probs * (prob_grad - weighted)).astype(BF16)
        value_part = dot_nn(probs.astype(BF16), grad)
        key_part = dot_nn(score_grad, query)
        if start == 0:
            value_total[...] = value_part
            key_total[...] = key_part
        else:
            value_total[...] += value_part
            key_total[...] += key_part
        out_ref[rows, :DH] = (dot_tn(score_grad, keys) * DH**-0.5).astype(BF16)
    out_ref[:, DH : 2 * DH] = (key_total[...] * DH**-0.5).astype(BF16)
    out_ref[:, 2 * DH :] = value_total[...].astype(BF16)


def attention_forward(qkv, seg_col, seg_row):
    length, width = qkv.shape
    heads = width // (3 * DH)
    return pl.pallas_call(
        functools.partial(attention_forward_kernel, block=min(256, length)),
        out_shape=jax.ShapeDtypeStruct((length, heads * DH), BF16),
        grid=(heads,),
        in_specs=[
            pl.BlockSpec((length, 3 * DH), lambda i: (0, i)),
            pl.BlockSpec((length, 1), lambda i: (0, 0)),
            pl.BlockSpec((1, length), lambda i: (0, 0)),
        ],
        out_specs=pl.BlockSpec((length, DH), lambda i: (0, i)),
        cost_estimate=pl.CostEstimate(
            flops=4 * heads * length * length * DH,
            transcendentals=heads * length * length,
            bytes_accessed=2 * length * heads * DH * 4,
        ),
        name="attention_forward",
    )(qkv, seg_col, seg_row)


def attention_backward(qkv, grad, seg_col, seg_row):
    length, width = qkv.shape
    heads = width // (3 * DH)
    return pl.pallas_call(
        functools.partial(attention_backward_kernel, block=min(256, length)),
        out_shape=jax.ShapeDtypeStruct((length, width), BF16),
        grid=(heads,),
        in_specs=[
            pl.BlockSpec((length, 3 * DH), lambda i: (0, i)),
            pl.BlockSpec((length, DH), lambda i: (0, i)),
            pl.BlockSpec((length, 1), lambda i: (0, 0)),
            pl.BlockSpec((1, length), lambda i: (0, 0)),
        ],
        out_specs=pl.BlockSpec((length, 3 * DH), lambda i: (0, i)),
        scratch_shapes=[pltpu.VMEM((length, DH), F32), pltpu.VMEM((length, DH), F32)],
        cost_estimate=pl.CostEstimate(
            flops=10 * heads * length * length * DH,
            transcendentals=heads * length * length,
            bytes_accessed=2 * length * heads * DH * 7,
        ),
        name="attention_backward",
    )(qkv, grad, seg_col, seg_row)


def reorder_kernel(mask_ref, in_ref, out_ref):
    out_ref[...] = in_ref[...]


def reorder(array, mask, count):
    rows, width = array.shape
    return pl.pallas_call(
        reorder_kernel,
        out_shape=jax.ShapeDtypeStruct(array.shape, array.dtype),
        grid_spec=pltpu.PrefetchScalarGridSpec(
            num_scalar_prefetch=1,
            grid=(count,),
            in_specs=[pl.BlockSpec((rows, width // count), lambda i, m: (0, i ^ m[0]))],
            out_specs=pl.BlockSpec((rows, width // count), lambda i, m: (0, i)),
        ),
        cost_estimate=pl.CostEstimate(
            flops=0, transcendentals=0, bytes_accessed=4 * rows * width
        ),
        name="reorder",
    )(mask, array)


def norm_forward(values, gain, shift):
    average = jnp.mean(values, axis=-1, keepdims=True)
    centered = values - average
    inverse = lax.rsqrt(jnp.mean(centered * centered, axis=-1, keepdims=True) + EPSILON)
    unit = centered * inverse
    return unit * gain + shift, unit, inverse


def norm_backward(grad, unit, inverse, gain):
    scaled = grad * gain
    first = jnp.mean(scaled, axis=-1, keepdims=True)
    second = jnp.mean(scaled * unit, axis=-1, keepdims=True)
    terms = (jnp.sum(grad * unit, axis=0), jnp.sum(grad, axis=0))
    return (scaled - first - unit * second) * inverse, terms


def gelu_pair(values):
    root = 0.7978845608028654
    square = values * values
    inner = jnp.tanh(root * values * (1.0 + 0.044715 * square))
    half = 0.5 * (1.0 + inner)
    slope = half + 0.5 * values * (1.0 - inner * inner) * root * (1.0 + 3 * 0.044715 * square)
    return values * half, slope


def per_device(
    tokens,
    segments,
    query_weight,
    key_weight,
    value_weight,
    output_weight,
    expand_weight,
    contract_weight,
    norm_gains,
    norm_shifts,
    cotangent,
):
    dp_size = lax.axis_size("dp")
    tensor_size = lax.axis_size("tensor")
    halves = tokens.shape[0]
    tp = tensor_size // halves
    total = dp_size * tensor_size
    block_tokens, width = tokens.shape[1], tokens.shape[2]
    blocks = dp_size
    chips = dp_size // 2
    local_width = query_weight.shape[1]
    heads = local_width // DH
    core_bit, half_bit = tensor_size, tp
    t_bits = [1 << i for i in range(tp.bit_length() - 1)]
    p_bits = [1 << i for i in range(chips.bit_length() - 1)]
    orders = (p_bits, p_bits[::-1])
    dp_index, tensor_index = lax.axis_index("dp"), lax.axis_index("tensor")
    p, c = dp_index // 2, dp_index % 2
    h, t = tensor_index // tp, tensor_index % tp
    basis = p * 2 + h
    basis_ref = basis.astype(jnp.int32).reshape(1)
    home = c * tp + t

    def swap(array, mask):
        return lax.ppermute(array, AXES, [(i, i ^ mask) for i in range(total)])

    def turned(j, back):
        pairs = []
        for i in range(total):
            it = i % tp
            ih = i // tp % halves
            ic = i // tensor_size % 2
            ip = i // tensor_size // 2
            to = ((ip * 2 + ih) * halves + (j ^ ic)) * tp + it
            pairs.append((to, i) if back else (i, to))
        return pairs

    def turn(array, j):
        return lax.ppermute(array, AXES, turned(j, False))

    def turn_back(array, j):
        return lax.ppermute(array, AXES, turned(j, True))

    def fetch(shard, axis):
        found = {}
        for j in range(2):
            own = {0: turn(shard, j)}
            for bit in orders[j]:
                own.update({k | bit: swap(v, bit * 2 * tensor_size) for k, v in own.items()})
            found.update({k * 2 + j: v for k, v in own.items()})
        return jnp.concatenate([found[b] for b in range(blocks)], axis=axis)

    def reduce_grad(pieces):
        sums = []
        for j in range(2):
            own = {k: pieces[k * 2 + j] for k in range(chips)}
            for bit in orders[j][::-1]:
                kept = {}
                for k in own:
                    if not k & bit:
                        got = swap(own[k | bit], bit * 2 * tensor_size)
                        kept[k] = (own[k].astype(F32) + got.astype(F32)).astype(BF16)
                own = kept
            sums.append(turn_back(own[0], j))
        return sums[0].astype(F32) + sums[1].astype(F32)

    def row_pieces(array):
        size = array.shape[0] // blocks
        return [array[b * size : (b + 1) * size] for b in range(blocks)]

    def column_pieces(array):
        size = array.shape[1] // blocks
        return [array[:, b * size : (b + 1) * size] for b in range(blocks)]

    def gather_rows(array):
        parts = [array]
        for bit in t_bits:
            parts = parts + [swap(part, bit) for part in parts]
        parts = parts + [swap(part, core_bit) for part in parts]
        return jnp.concatenate(parts, axis=0)

    def reduce_rows(array):
        array = array.astype(BF16)
        middle = array.shape[0] // 2
        kept = array[:middle].astype(F32) + swap(array[middle:], core_bit).astype(F32)
        for bit in t_bits[::-1]:
            middle = kept.shape[0] // 2
            kept = kept[:middle] + swap(kept[middle:].astype(BF16), bit).astype(F32)
        return kept

    own_params = jnp.concatenate([norm_gains, norm_shifts], axis=0)
    other_params = swap(own_params, core_bit)
    pair = [jnp.where((h ^ j) == c, own_params, other_params) for j in range(2)]
    found = {0: jnp.stack(pair, axis=1)}
    for bit in p_bits:
        found.update({k | bit: swap(v, bit * 2 * tensor_size) for k, v in found.items()})
    params = jnp.stack([found[k] for k in range(chips)], axis=1).reshape(4, width).astype(F32)
    gains, shifts = params[:2], params[2:]

    own_segments = jnp.where(h == 0, segments[0, 0], segments[1, 0])
    other_segments = swap(own_segments, core_bit)

    def segments_of(j):
        row = jnp.where((h ^ j) == c, own_segments, other_segments)
        row = row.reshape(2 * tp, block_tokens)
        bits = [tp] + t_bits
        for bit in bits:
            moved = row.reshape(2 * tp // (2 * bit), 2, bit, block_tokens)
            moved = jnp.concatenate([moved[:, 1:], moved[:, :1]], axis=1)
            row = jnp.where((home & bit) != 0, moved.reshape(row.shape), row)
        row = row.reshape(-1)
        return row[:, None], row[None, :]

    def to_home(array, j):
        piece = jnp.where((j ^ c) == 0, array[0], array[1])
        return reorder(turn(piece, j), basis_ref, blocks)

    def from_home(pieces):
        back = [turn_back(reorder(piece, basis_ref, blocks), j) for j, piece in enumerate(pieces)]
        return jnp.stack(
            [jnp.where(c == 0, back[0], back[1]), jnp.where(c == 0, back[1], back[0])]
        )

    streams = range(2)
    homes = [to_home(tokens, j) for j in streams]
    rows = [gather_rows(x) for x in homes]

    shard = jnp.stack(
        [w.reshape(-1, heads, DH) for w in (query_weight, key_weight, value_weight)], axis=2
    ).reshape(-1, 3 * local_width)
    full_qkv = fetch(shard, 0)
    full_output = fetch(output_weight, 1)
    full_expand = fetch(expand_weight, 0)
    full_contract = fetch(contract_weight, 1)
    segs = [segments_of(j) for j in streams]
    grads_home = [to_home(cotangent, j) for j in streams]

    qkv = [dot_nn(x, full_qkv).astype(BF16) for x in rows]
    context = [attention_forward(qkv[j], *segs[j]) for j in streams]
    first = [
        norm_forward(
            homes[j].astype(F32) + reduce_rows(dot_nn(context[j], full_output)), gains[0], shifts[0]
        )
        for j in streams
    ]
    normed_rows = [gather_rows(first[j][0].astype(BF16)) for j in streams]
    active, slope = [], []
    for j in streams:
        value, derivative = gelu_pair(dot_nn(normed_rows[j], full_expand))
        active.append(value.astype(BF16))
        slope.append(derivative.astype(BF16))
    second = [
        norm_forward(
            first[j][0] + reduce_rows(dot_nn(active[j], full_contract)), gains[1], shifts[1]
        )
        for j in streams
    ]
    result = from_home([second[j][0].astype(BF16) for j in streams])

    branch_grad = [
        norm_backward(grads_home[j].astype(F32), second[j][1], second[j][2], gains[1])
        for j in streams
    ]
    branch_rows = [gather_rows(branch_grad[j][0].astype(BF16)) for j in streams]
    hidden_grad = [
        (dot_nt(branch_rows[j], full_contract) * slope[j].astype(F32)).astype(BF16)
        for j in streams
    ]
    normed_grad = [
        branch_grad[j][0] + reduce_rows(dot_nt(hidden_grad[j], full_expand)) for j in streams
    ]
    contract_grad = sum(dot_tn(active[j], branch_rows[j]) for j in streams).astype(BF16)
    contract_grad = reduce_grad(column_pieces(contract_grad))
    expand_grad = sum(dot_tn(normed_rows[j], hidden_grad[j]) for j in streams).astype(BF16)
    expand_grad = reduce_grad(row_pieces(expand_grad))

    first_grad = [
        norm_backward(normed_grad[j], first[j][1], first[j][2], gains[0]) for j in streams
    ]
    attended_rows = [gather_rows(first_grad[j][0].astype(BF16)) for j in streams]
    output_grad = sum(dot_tn(context[j], attended_rows[j]) for j in streams).astype(BF16)
    output_grad = reduce_grad(column_pieces(output_grad))
    context_grad = [dot_nt(attended_rows[j], full_output).astype(BF16) for j in streams]
    qkv_grad = [attention_backward(qkv[j], context_grad[j], *segs[j]) for j in streams]
    projection_grad = sum(dot_tn(rows[j], qkv_grad[j]) for j in streams).astype(BF16)
    projection_grad = reduce_grad(row_pieces(projection_grad))
    projection_grad = projection_grad.reshape(-1, heads, 3, DH)
    query_grad, key_grad, value_grad = [
        projection_grad[:, :, i].reshape(-1, local_width) for i in range(3)
    ]
    tokens_grad = from_home(
        [
            (first_grad[j][0] + reduce_rows(dot_nt(qkv_grad[j], full_qkv))).astype(BF16)
            for j in streams
        ]
    ).astype(F32)

    terms = jnp.stack(
        [
            sum(first_grad[j][1][0] for j in streams),
            sum(branch_grad[j][1][0] for j in streams),
            sum(first_grad[j][1][1] for j in streams),
            sum(branch_grad[j][1][1] for j in streams),
        ]
    )
    for bit in t_bits + [core_bit]:
        terms = terms + swap(terms, bit)
    terms = terms.reshape(4, chips, 2, -1)
    for bit in p_bits[::-1]:
        middle = terms.shape[1] // 2
        terms = terms[:, :middle] + swap(terms[:, middle:], bit * 2 * tensor_size)
    terms = turn_back(terms[:, 0, 0], 0) + turn_back(terms[:, 0, 1], 1)

    return (
        result,
        tokens_grad,
        query_grad,
        key_grad,
        value_grad,
        output_grad,
        expand_grad,
        contract_grad,
        terms[:2],
        terms[2:],
    )


def solution(mesh):
    in_specs = (
        P(None, ("dp", "tensor"), None),
        P(None, "dp", None),
        P("dp", "tensor"),
        P("dp", "tensor"),
        P("dp", "tensor"),
        P("tensor", "dp"),
        P("dp", "tensor"),
        P("tensor", "dp"),
        P(None, "dp"),
        P(None, "dp"),
        P(None, ("dp", "tensor"), None),
    )
    out_specs = (
        P(None, ("dp", "tensor"), None),
        P(None, ("dp", "tensor"), None),
        P("dp", "tensor"),
        P("dp", "tensor"),
        P("dp", "tensor"),
        P("tensor", "dp"),
        P("dp", "tensor"),
        P("tensor", "dp"),
        P(None, "dp"),
        P(None, "dp"),
    )
    return jax.shard_map(
        per_device, mesh=mesh, in_specs=in_specs, out_specs=out_specs, check_vma=False
    )
```

```python
import functools

import jax
import jax.numpy as jnp
from jax import lax
from jax.experimental import pallas as pl
from jax.experimental.pallas import tpu as pltpu
from jax.sharding import PartitionSpec as P

DH = 128
EPSILON = 1e-06
NEGATIVE = -1e30
AXES = ("dp", "tensor")
F32 = jnp.float32
BF16 = jnp.bfloat16


def dot_nn(left, right):
    return jnp.dot(left, right, preferred_element_type=F32)


def dot_tn(left, right):
    return lax.dot_general(left, right, (((0,), (0,)), ((), ())), preferred_element_type=F32)


def dot_nt(left, right):
    return lax.dot_general(left, right, (((1,), (1,)), ((), ())), preferred_element_type=F32)


def attention_forward_kernel(qkv_ref, seg_col_ref, seg_row_ref, out_ref, *, block):
    length = qkv_ref.shape[0]
    keys = qkv_ref[:, DH : 2 * DH]
    values = qkv_ref[:, 2 * DH :]
    seg_row = seg_row_ref[...]
    for start in range(0, length, block):
        rows = slice(start, start + block)
        scores = dot_nt(qkv_ref[rows, :DH], keys)
        scores = jnp.where(seg_col_ref[rows, :] == seg_row, scores, NEGATIVE)
        top = jnp.max(scores, axis=1, keepdims=True)
        exponent = jnp.exp((scores - top) * DH**-0.5)
        total = jnp.sum(exponent, axis=1, keepdims=True)
        context = dot_nn(exponent.astype(BF16), values)
        out_ref[rows, :] = (context / total).astype(BF16)


def attention_backward_kernel(
    qkv_ref, grad_ref, seg_col_ref, seg_row_ref, out_ref, key_total, value_total, *, block
):
    length = qkv_ref.shape[0]
    keys = qkv_ref[:, DH : 2 * DH]
    values = qkv_ref[:, 2 * DH :]
    seg_col = seg_col_ref[...]
    for start in range(0, length, block):
        rows = slice(start, start + block)
        query = qkv_ref[rows, :DH]
        grad = grad_ref[rows, :]
        scores = dot_nt(keys, query)
        scores = jnp.where(seg_col == seg_row_ref[:, rows], scores, NEGATIVE)
        top = jnp.max(scores, axis=0, keepdims=True)
        exponent = jnp.exp((scores - top) * DH**-0.5)
        probs = exponent * (1.0 / jnp.sum(exponent, axis=0, keepdims=True))
        prob_grad = dot_nt(values, grad)
        weighted = jnp.sum(probs * prob_grad, axis=0, keepdims=True)
        score_grad = (probs * (prob_grad - weighted)).astype(BF16)
        value_part = dot_nn(probs.astype(BF16), grad)
        key_part = dot_nn(score_grad, query)
        if start == 0:
            value_total[...] = value_part
            key_total[...] = key_part
        else:
            value_total[...] += value_part
            key_total[...] += key_part
        out_ref[rows, :DH] = (dot_tn(score_grad, keys) * DH**-0.5).astype(BF16)
    out_ref[:, DH : 2 * DH] = (key_total[...] * DH**-0.5).astype(BF16)
    out_ref[:, 2 * DH :] = value_total[...].astype(BF16)


def attention_forward(qkv, seg_col, seg_row):
    length, width = qkv.shape
    heads = width // (3 * DH)
    return pl.pallas_call(
        functools.partial(attention_forward_kernel, block=min(256, length)),
        out_shape=jax.ShapeDtypeStruct((length, heads * DH), BF16),
        grid=(heads,),
        in_specs=[
            pl.BlockSpec((length, 3 * DH), lambda i: (0, i)),
            pl.BlockSpec((length, 1), lambda i: (0, 0)),
            pl.BlockSpec((1, length), lambda i: (0, 0)),
        ],
        out_specs=pl.BlockSpec((length, DH), lambda i: (0, i)),
        cost_estimate=pl.CostEstimate(
            flops=4 * heads * length * length * DH,
            transcendentals=heads * length * length,
            bytes_accessed=2 * length * heads * DH * 4,
        ),
        name="attention_forward",
    )(qkv, seg_col, seg_row)


def attention_backward(qkv, grad, seg_col, seg_row):
    length, width = qkv.shape
    heads = width // (3 * DH)
    return pl.pallas_call(
        functools.partial(attention_backward_kernel, block=min(256, length)),
        out_shape=jax.ShapeDtypeStruct((length, width), BF16),
        grid=(heads,),
        in_specs=[
            pl.BlockSpec((length, 3 * DH), lambda i: (0, i)),
            pl.BlockSpec((length, DH), lambda i: (0, i)),
            pl.BlockSpec((length, 1), lambda i: (0, 0)),
            pl.BlockSpec((1, length), lambda i: (0, 0)),
        ],
        out_specs=pl.BlockSpec((length, 3 * DH), lambda i: (0, i)),
        scratch_shapes=[pltpu.VMEM((length, DH), F32), pltpu.VMEM((length, DH), F32)],
        cost_estimate=pl.CostEstimate(
            flops=10 * heads * length * length * DH,
            transcendentals=heads * length * length,
            bytes_accessed=2 * length * heads * DH * 7,
        ),
        name="attention_backward",
    )(qkv, grad, seg_col, seg_row)


def reorder_kernel(mask_ref, in_ref, out_ref):
    out_ref[...] = in_ref[...]


def reorder(array, table):
    rows, width = array.shape
    count = table.shape[0]
    return pl.pallas_call(
        reorder_kernel,
        out_shape=jax.ShapeDtypeStruct(array.shape, array.dtype),
        grid_spec=pltpu.PrefetchScalarGridSpec(
            num_scalar_prefetch=1,
            grid=(count,),
            in_specs=[pl.BlockSpec((rows, width // count), lambda i, m: (0, m[i]))],
            out_specs=pl.BlockSpec((rows, width // count), lambda i, m: (0, i)),
        ),
        cost_estimate=pl.CostEstimate(
            flops=0, transcendentals=0, bytes_accessed=4 * rows * width
        ),
        name="reorder",
    )(table, array)


def norm_forward(values, gain, shift):
    average = jnp.mean(values, axis=-1, keepdims=True)
    centered = values - average
    inverse = lax.rsqrt(jnp.mean(centered * centered, axis=-1, keepdims=True) + EPSILON)
    unit = centered * inverse
    return unit * gain + shift, unit, inverse


def norm_backward(grad, unit, inverse, gain):
    scaled = grad * gain
    first = jnp.mean(scaled, axis=-1, keepdims=True)
    second = jnp.mean(scaled * unit, axis=-1, keepdims=True)
    terms = (jnp.sum(grad * unit, axis=0), jnp.sum(grad, axis=0))
    return (scaled - first - unit * second) * inverse, terms


def gelu_pair(values):
    root = 0.7978845608028654
    square = values * values
    inner = jnp.tanh(root * values * (1.0 + 0.044715 * square))
    half = 0.5 * (1.0 + inner)
    slope = half + 0.5 * values * (1.0 - inner * inner) * root * (1.0 + 3 * 0.044715 * square)
    return values * half, slope


def per_device(
    tokens,
    segments,
    query_weight,
    key_weight,
    value_weight,
    output_weight,
    expand_weight,
    contract_weight,
    norm_gains,
    norm_shifts,
    cotangent,
):
    dp_size = lax.axis_size("dp")
    tensor_size = lax.axis_size("tensor")
    halves = tokens.shape[0]
    tp = tensor_size // halves
    total = dp_size * tensor_size
    block_tokens, width = tokens.shape[1], tokens.shape[2]
    blocks = dp_size
    chips = dp_size // 2
    local_width = query_weight.shape[1]
    heads = local_width // DH
    core_bit, half_bit = tensor_size, tp
    t_bits = [1 << i for i in range(tp.bit_length() - 1)]
    p_bits = [1 << i for i in range(chips.bit_length() - 1)]
    orders = (p_bits, p_bits[::-1])
    dp_index, tensor_index = lax.axis_index("dp"), lax.axis_index("tensor")
    p, c = dp_index // 2, dp_index % 2
    h, t = tensor_index // tp, tensor_index % tp
    basis = (p * 2 + h).astype(jnp.int32)

    def reversed_bits(k):
        return sum(((k // bit) % 2) * (chips // 2 // bit) for bit in p_bits)

    def place(block):
        k, j = block // 2, block % 2
        return j * chips + jnp.where(j == 0, k, reversed_bits(k))

    numbers = jnp.arange(blocks, dtype=jnp.int32)
    rank = numbers % chips
    to_table = (
        jnp.where(numbers < chips, rank * 2, reversed_bits(rank) * 2 + 1).astype(jnp.int32) ^ basis
    )
    from_table = place(numbers ^ basis).astype(jnp.int32)
    home = c * tp + t

    def swap(array, mask):
        return lax.ppermute(array, AXES, [(i, i ^ mask) for i in range(total)])

    same = c == h

    def after(array, *others):
        return lax.optimization_barrier((array, *others))[0]


    def near(shard, other):
        got = swap(jnp.where(same, other, shard), core_bit)
        return [jnp.where(same, shard, got), jnp.where(same, got, other)]

    def moved(parts, step):
        got = [swap(v, order[step] * 2 * tensor_size) for v, order in zip(parts, orders)]
        return list(lax.optimization_barrier(tuple(got)))

    def joined(parts, got, axis):
        return [jnp.concatenate([v, w], axis=axis) for v, w in zip(parts, got)]

    def doubled(parts, axis, begin, end):
        for step in range(begin, end):
            parts = joined(parts, moved(parts, step), axis)
        return parts

    def tied(parts, *others):
        return list(lax.optimization_barrier((*parts, *others)))[: len(parts)]

    last = len(p_bits) - 1


    def split_send(parts, step, axis):
        halves_of = [jnp.split(v, 2, axis=axis) for v in parts]
        got = [
            swap(v[1], order[step] * 2 * tensor_size) for v, order in zip(halves_of, orders)
        ]
        return [v[0] for v in halves_of], list(lax.optimization_barrier(tuple(got)))

    def added(kept, got):
        return [(v.astype(F32) + w.astype(F32)).astype(BF16) for v, w in zip(kept, got)]

    def collect(first, second):
        got = swap(jnp.where(same, second, first), core_bit)
        kept = jnp.where(same, first, got)
        return kept, swap(jnp.where(same, got, second), half_bit)

    def reduce_rest(parts, axis, step):
        for s in range(step, -1, -1):
            parts = added(*split_send(parts, s, axis))
        kept, got = collect(*parts)
        return kept, got

    def total_of(kept, got):
        return kept.astype(F32) + got.astype(F32)


    def gather_far(array):
        parts = [array]
        for bit in t_bits:
            parts = parts + [swap(part, bit) for part in parts]
        return parts

    def gather_near(parts):
        return jnp.concatenate(parts + [swap(part, core_bit) for part in parts], axis=0)

    def gather_rows(array):
        return gather_near(gather_far(array))

    def reduce_near(array):
        array = array.astype(BF16)
        middle = array.shape[0] // 2
        return array[:middle].astype(F32) + swap(array[middle:], core_bit).astype(F32)

    def reduce_far(kept):
        for bit in t_bits[:0:-1]:
            middle = kept.shape[0] // 2
            kept = kept[:middle] + swap(kept[middle:].astype(BF16), bit).astype(F32)
        middle = kept.shape[0] // 2
        return kept[:middle], swap(kept[middle:].astype(BF16), t_bits[0])

    def ready(pair, *others):
        return pair[0] + after(pair[1], *others).astype(F32)

    own_segments = jnp.where(h == 0, segments[0, 0], segments[1, 0])
    other_segments = swap(own_segments, core_bit)

    def segments_of(j):
        row = jnp.where((h ^ j) == c, own_segments, other_segments)
        row = row.reshape(2 * tp, block_tokens)
        bits = [tp] + t_bits
        for bit in bits:
            moved = row.reshape(2 * tp // (2 * bit), 2, bit, block_tokens)
            moved = jnp.concatenate([moved[:, 1:], moved[:, :1]], axis=1)
            row = jnp.where((home & bit) != 0, moved.reshape(row.shape), row)
        row = row.reshape(-1)
        return row[:, None], row[None, :]

    def parted(array):
        return jnp.where(h == 0, array[0], array[1]), jnp.where(h == 0, array[1], array[0])

    def to_home(own, other):
        got = swap(jnp.where(same, other, own), core_bit)
        pair = [jnp.where(same, own, got), jnp.where(same, got, other)]
        both = reorder(jnp.concatenate(pair, axis=0), to_table)
        return [both[:block_tokens], both[block_tokens:]]

    def sent_home(pieces):
        both = reorder(jnp.concatenate(pieces, axis=0), from_table)
        return collect(both[:block_tokens], both[block_tokens:])

    def home_pair(kept, got):
        return jnp.stack([jnp.where(h == 0, kept, got), jnp.where(h == 0, got, kept)])

    streams = range(2)
    extra = 16
    qkv_shard = jnp.stack(
        [w.reshape(-1, heads, DH) for w in (query_weight, key_weight, value_weight)], axis=2
    ).reshape(-1, 3 * local_width)
    params = jnp.concatenate([norm_gains, norm_shifts], axis=0)
    params = jnp.pad(params, ((0, extra - params.shape[0]), (0, 0)))
    output_shard = jnp.concatenate([output_weight, params], axis=0)

    qkv_other = swap(qkv_shard, half_bit)
    token_own, token_send = parted(tokens)
    token_other = swap(after(token_send, qkv_other), half_bit)
    qkv_parts = doubled(near(qkv_shard, qkv_other), 0, 0, 1)
    token_other = after(token_other, *qkv_parts)
    qkv_parts = tied(qkv_parts, token_other)
    output_other = swap(after(output_shard, token_other), half_bit)
    expand_other = swap(after(expand_weight, token_other), half_bit)
    homes = to_home(token_own, token_other)
    sent = [gather_far(homes[0])]
    sent.append(gather_far(after(homes[1], *sent[0])))
    qkv_parts = doubled(qkv_parts, 0, 1, last)
    qkv_got = moved(qkv_parts, last)
    full_qkv = jnp.concatenate([qkv_parts[0], qkv_got[0], qkv_parts[1], qkv_got[1]], axis=0)
    output_other = after(output_other, full_qkv, sent[0][-1])
    output_parts = doubled(near(output_shard, output_other), 1, 0, last + 1)
    segs = [segments_of(j) for j in streams]

    rows = [gather_near(sent[0])]
    qkv = [dot_nn(rows[0], full_qkv).astype(BF16)]
    context = [attention_forward(qkv[0], *segs[0])]
    full_output = jnp.concatenate([x[:local_width] for x in output_parts], axis=1)
    params = jnp.concatenate([x[local_width : local_width + 4] for x in output_parts], axis=1)
    params = params.astype(F32)
    gains, shifts = params[:2], params[2:]
    partial = [reduce_near(dot_nn(context[0], full_output))]
    attended = [reduce_far(partial[0])]
    expand_other = after(expand_other, partial[0])
    contract_other = swap(after(contract_weight, expand_other), half_bit)
    expand_parts = doubled(near(expand_weight, expand_other), 0, 0, last)
    rows.append(gather_near(tied(sent[1], partial[0])))
    qkv.append(dot_nn(rows[1], full_qkv).astype(BF16))
    context.append(attention_forward(qkv[1], *segs[1]))
    expand_got = moved(tied(expand_parts, context[1]), last)

    partial.append(reduce_near(dot_nn(context[1], full_output)))
    attended.append(reduce_far(partial[1]))
    first = [
        norm_forward(homes[0].astype(F32) + ready(attended[0], partial[1]), gains[0], shifts[0])
    ]
    normed = [first[0][0].astype(BF16)]
    sent = [gather_far(normed[0])]
    contract_other = after(contract_other, normed[0])
    first.append(
        norm_forward(
            homes[1].astype(F32) + ready(attended[1], contract_other), gains[0], shifts[0]
        )
    )
    normed.append(first[1][0].astype(BF16))
    sent.append(gather_far(normed[1]))
    cotangent_own, cotangent_send = parted(cotangent)
    cotangent_other = swap(after(cotangent_send, contract_other), half_bit)
    contract_parts = near(contract_weight, contract_other)
    expand_got = tied(expand_got, normed[1])
    full_expand = jnp.concatenate(
        [expand_parts[0], expand_got[0], expand_parts[1], expand_got[1]], axis=0
    )
    contract_parts = doubled(tied(contract_parts, *expand_got), 1, 0, last)
    normed_rows, active, slope, branch = [], [], [], []
    gate = tuple(contract_parts)
    for j in streams:
        normed_rows.append(after(gather_near(sent[j]), *gate))
        value, derivative = gelu_pair(dot_nn(normed_rows[j], full_expand))
        active.append(value.astype(BF16))
        slope.append(derivative.astype(BF16))
        gate = (active[j],)
    contract_got = tied(moved(contract_parts, last), active[1])
    full_contract = jnp.concatenate(
        [contract_parts[0], contract_got[0], contract_parts[1], contract_got[1]], axis=1
    )
    grads_home = to_home(cotangent_own, after(cotangent_other, active[1]))
    partial, pairs = [], []
    gate = (active[1],)
    for j in streams:
        branch.append(dot_nn(after(active[j], *gate), full_contract).astype(BF16))
        partial.append(reduce_near(branch[j]))
        pairs.append(reduce_far(partial[j]))
        gate = (branch[j],)

    second, branch_grad, sent = [], [], []
    gate = (partial[1], *grads_home)
    for j in streams:
        second.append(norm_forward(first[j][0] + ready(pairs[j], *gate), gains[1], shifts[1]))
        branch_grad.append(
            norm_backward(grads_home[j].astype(F32), second[j][1], second[j][2], gains[1])
        )
        gate = (branch_grad[j][0].astype(BF16),)
        sent.append(gather_far(gate[0]))
    branch_rows, hidden_grad, normed_part = [], [], []
    partial, pairs = [], []
    for j in streams:
        branch_rows.append(after(gather_near(sent[j]), *gate))
        hidden_grad.append(
            (dot_nt(branch_rows[j], full_contract) * slope[j].astype(F32)).astype(BF16)
        )
        normed_part.append(dot_nt(hidden_grad[j], full_expand).astype(BF16))
        partial.append(reduce_near(normed_part[j]))
        pairs.append(reduce_far(partial[j]))
        gate = (partial[j],)
    result_kept, result_got = sent_home(
        [after(second[j][0].astype(BF16), branch_rows[1]) for j in streams]
    )
    tied_active = after(active[0], *gate)
    contract_grad = dot_tn(tied_active, branch_rows[0]) + dot_tn(active[1], branch_rows[1])
    contract_grad = contract_grad.astype(BF16)
    contract_kept, contract_got = split_send(jnp.split(contract_grad, 2, axis=1), last, 1)
    normed_grad = [branch_grad[0][0] + ready(pairs[0], contract_grad)]
    first_grad = [norm_backward(normed_grad[0], first[0][1], first[0][2], gains[0])]
    gate = first_grad[0][0].astype(BF16)
    sent = [gather_far(gate)]
    tied_normed = after(normed_rows[0], gate)
    expand_grad = dot_tn(tied_normed, hidden_grad[0]) + dot_tn(normed_rows[1], hidden_grad[1])
    expand_grad = expand_grad.astype(BF16)
    result_got = after(result_got, expand_grad)
    result = home_pair(result_kept, result_got)
    normed_grad.append(branch_grad[1][0] + ready(pairs[1], expand_grad))
    first_grad.append(norm_backward(normed_grad[1], first[1][1], first[1][2], gains[0]))
    sent.append(gather_far(first_grad[1][0].astype(BF16)))
    contract_got = tied(contract_got, expand_grad, sent[1][0])
    contract_kept, contract_got = split_send(added(contract_kept, contract_got), last - 1, 1)
    expand_kept, expand_got = split_send(
        tied(jnp.split(expand_grad, 2, axis=0), *contract_kept), last, 0
    )

    terms = jnp.stack(
        [
            sum(first_grad[j][1][0] for j in streams),
            sum(branch_grad[j][1][0] for j in streams),
            sum(first_grad[j][1][1] for j in streams),
            sum(branch_grad[j][1][1] for j in streams),
        ]
    )

    attended_rows = [after(gather_near(sent[0]), expand_grad, sent[1][0])]
    context_grad = dot_nt(attended_rows[0], full_output).astype(BF16)
    qkv_grad = [attention_backward(qkv[0], context_grad, *segs[0])]
    partial = [reduce_near(dot_nt(qkv_grad[0], full_qkv).astype(BF16))]
    pairs = [reduce_far(partial[0])]
    attended_rows.append(after(gather_near(tied(sent[1], qkv_grad[0])), partial[0]))
    contract_kept, contract_got = reduce_rest(
        added(contract_kept, tied(contract_got, qkv_grad[0])), 1, last - 2
    )
    terms = after(terms, qkv_grad[0])
    for bit in t_bits + [core_bit]:
        terms = terms + swap(terms, bit)
    terms = jnp.pad(terms, ((0, extra - 4), (0, 0)))
    output_grad = dot_tn(context[0], attended_rows[0]) + dot_tn(context[1], attended_rows[1])
    output_grad = jnp.concatenate([output_grad, terms], axis=0).astype(BF16)
    expand_kept, expand_got = split_send(
        added(expand_kept, tied(expand_got, output_grad)), last - 1, 0
    )
    context_grad = dot_nt(
        after(attended_rows[1], output_grad, contract_kept, *expand_kept), full_output
    ).astype(BF16)
    qkv_grad.append(attention_backward(qkv[1], context_grad, *segs[1]))
    expand_kept, expand_got = reduce_rest(
        added(expand_kept, tied(expand_got, qkv_grad[1])), 0, last - 2
    )
    contract_grad = total_of(contract_kept, after(contract_got, expand_kept))
    output_parts = jnp.split(output_grad, 2, axis=1)
    partial.append(reduce_near(dot_nt(qkv_grad[1], full_qkv).astype(BF16)))
    pairs.append(reduce_far(partial[1]))
    projection_grad = dot_tn(after(rows[0], partial[1], expand_kept), qkv_grad[0])
    projection_grad = (projection_grad + dot_tn(rows[1], qkv_grad[1])).astype(BF16)
    token_sums = [
        (first_grad[j][0] + ready(pairs[j], projection_grad)).astype(BF16) for j in streams
    ]
    output_grad = total_of(*reduce_rest(output_parts, 1, last))
    tokens_grad = home_pair(*sent_home(token_sums)).astype(F32)
    projection_grad = total_of(*reduce_rest(jnp.split(projection_grad, 2, axis=0), 0, last))
    expand_grad = total_of(expand_kept, expand_got)
    projection_grad = projection_grad.reshape(-1, heads, 3, DH)
    query_grad, key_grad, value_grad = [
        projection_grad[:, :, i].reshape(-1, local_width) for i in range(3)
    ]

    return (
        result,
        tokens_grad,
        query_grad,
        key_grad,
        value_grad,
        output_grad[:local_width],
        expand_grad,
        contract_grad,
        output_grad[local_width : local_width + 2],
        output_grad[local_width + 2 : local_width + 4],
    )


def solution(mesh):
    in_specs = (
        P(None, ("dp", "tensor"), None),
        P(None, "dp", None),
        P("dp", "tensor"),
        P("dp", "tensor"),
        P("dp", "tensor"),
        P("tensor", "dp"),
        P("dp", "tensor"),
        P("tensor", "dp"),
        P(None, "dp"),
        P(None, "dp"),
        P(None, ("dp", "tensor"), None),
    )
    out_specs = (
        P(None, ("dp", "tensor"), None),
        P(None, ("dp", "tensor"), None),
        P("dp", "tensor"),
        P("dp", "tensor"),
        P("dp", "tensor"),
        P("tensor", "dp"),
        P("dp", "tensor"),
        P("tensor", "dp"),
        P(None, "dp"),
        P(None, "dp"),
    )
    return jax.shard_map(
        per_device, mesh=mesh, in_specs=in_specs, out_specs=out_specs, check_vma=False
    )
```

```python
import functools

import jax
import jax.numpy as jnp
from jax import lax
from jax.experimental import pallas as pl
from jax.experimental.pallas import tpu as pltpu
from jax.sharding import PartitionSpec as P

DH = 128
EPSILON = 1e-06
NEGATIVE = -1e30
AXES = ("dp", "tensor")
HINT = 1 << 16
F32 = jnp.float32
BF16 = jnp.bfloat16


def dot_nn(left, right):
    return jnp.dot(left, right, preferred_element_type=F32)


def dot_tn(left, right):
    return lax.dot_general(left, right, (((0,), (0,)), ((), ())), preferred_element_type=F32)


def dot_nt(left, right):
    return lax.dot_general(left, right, (((1,), (1,)), ((), ())), preferred_element_type=F32)


def attention_forward_kernel(qkv_ref, seg_col_ref, seg_row_ref, out_ref, *, block):
    length = qkv_ref.shape[0]
    keys = qkv_ref[:, DH : 2 * DH]
    values = qkv_ref[:, 2 * DH :]
    seg_row = seg_row_ref[...]
    for start in range(0, length, block):
        rows = slice(start, start + block)
        scores = dot_nt(qkv_ref[rows, :DH], keys)
        scores = jnp.where(seg_col_ref[rows, :] == seg_row, scores, NEGATIVE)
        top = jnp.max(scores, axis=1, keepdims=True)
        exponent = jnp.exp((scores - top) * DH**-0.5)
        total = jnp.sum(exponent, axis=1, keepdims=True)
        context = dot_nn(exponent.astype(BF16), values)
        out_ref[rows, :] = (context / total).astype(BF16)


def attention_backward_kernel(
    qkv_ref, grad_ref, seg_col_ref, seg_row_ref, out_ref, key_total, value_total, *, block
):
    length = qkv_ref.shape[0]
    keys = qkv_ref[:, DH : 2 * DH]
    values = qkv_ref[:, 2 * DH :]
    seg_col = seg_col_ref[...]
    for start in range(0, length, block):
        rows = slice(start, start + block)
        query = qkv_ref[rows, :DH]
        grad = grad_ref[rows, :]
        scores = dot_nt(keys, query)
        scores = jnp.where(seg_col == seg_row_ref[:, rows], scores, NEGATIVE)
        top = jnp.max(scores, axis=0, keepdims=True)
        exponent = jnp.exp((scores - top) * DH**-0.5)
        probs = exponent * (1.0 / jnp.sum(exponent, axis=0, keepdims=True))
        prob_grad = dot_nt(values, grad)
        weighted = jnp.sum(probs * prob_grad, axis=0, keepdims=True)
        score_grad = (probs * (prob_grad - weighted)).astype(BF16)
        value_part = dot_nn(probs.astype(BF16), grad)
        key_part = dot_nn(score_grad, query)
        if start == 0:
            value_total[...] = value_part
            key_total[...] = key_part
        else:
            value_total[...] += value_part
            key_total[...] += key_part
        out_ref[rows, :DH] = (dot_tn(score_grad, keys) * DH**-0.5).astype(BF16)
    out_ref[:, DH : 2 * DH] = (key_total[...] * DH**-0.5).astype(BF16)
    out_ref[:, 2 * DH :] = value_total[...].astype(BF16)


def attention_forward(qkv, seg_col, seg_row):
    length, width = qkv.shape
    heads = width // (3 * DH)
    return pl.pallas_call(
        functools.partial(attention_forward_kernel, block=min(256, length)),
        out_shape=jax.ShapeDtypeStruct((length, heads * DH), BF16),
        grid=(heads,),
        in_specs=[
            pl.BlockSpec((length, 3 * DH), lambda i: (0, i)),
            pl.BlockSpec((length, 1), lambda i: (0, 0)),
            pl.BlockSpec((1, length), lambda i: (0, 0)),
        ],
        out_specs=pl.BlockSpec((length, DH), lambda i: (0, i)),
        cost_estimate=pl.CostEstimate(
            flops=HINT, transcendentals=0, bytes_accessed=HINT
        ),
        name="attention_forward",
    )(qkv, seg_col, seg_row)


def attention_backward(qkv, grad, seg_col, seg_row):
    length, width = qkv.shape
    heads = width // (3 * DH)
    return pl.pallas_call(
        functools.partial(attention_backward_kernel, block=min(256, length)),
        out_shape=jax.ShapeDtypeStruct((length, width), BF16),
        grid=(heads,),
        in_specs=[
            pl.BlockSpec((length, 3 * DH), lambda i: (0, i)),
            pl.BlockSpec((length, DH), lambda i: (0, i)),
            pl.BlockSpec((length, 1), lambda i: (0, 0)),
            pl.BlockSpec((1, length), lambda i: (0, 0)),
        ],
        out_specs=pl.BlockSpec((length, 3 * DH), lambda i: (0, i)),
        scratch_shapes=[pltpu.VMEM((length, DH), F32), pltpu.VMEM((length, DH), F32)],
        cost_estimate=pl.CostEstimate(
            flops=HINT, transcendentals=0, bytes_accessed=HINT
        ),
        name="attention_backward",
    )(qkv, grad, seg_col, seg_row)


def matmul_kernel(*refs, contract, finish, extras):
    left_ref, right_ref = refs[:2]
    product = lax.dot_general(
        left_ref[...], right_ref[...], (((1,), (contract,)), ((), ())), preferred_element_type=F32
    )
    results = finish(product, *[ref[...] for ref in refs[2 : 2 + extras]])
    for ref, value in zip(refs[2 + extras :], results):
        ref[...] = value.astype(ref.dtype)


def rounded(product):
    return (product,)


def matmul(left, right, transposed=False, finish=rounded, extras=(), outs=1, name="matmul"):
    rows, depth = left.shape
    columns = right.shape[0 if transposed else 1]
    block = min(512, columns)
    if transposed:
        right_spec = pl.BlockSpec((block, depth), lambda i: (i, 0))
    else:
        right_spec = pl.BlockSpec((depth, block), lambda i: (0, i))
    wide = pl.BlockSpec((rows, block), lambda i: (0, i))
    found = pl.pallas_call(
        functools.partial(
            matmul_kernel, contract=int(transposed), finish=finish, extras=len(extras)
        ),
        out_shape=[jax.ShapeDtypeStruct((rows, columns), BF16)] * outs,
        grid=(columns // block,),
        in_specs=[pl.BlockSpec((rows, depth), lambda i: (0, 0)), right_spec] + [wide] * len(extras),
        out_specs=[wide] * outs,
        cost_estimate=pl.CostEstimate(
            flops=HINT, transcendentals=0, bytes_accessed=HINT
        ),
        name=name,
    )(left, right, *extras)
    return found if outs > 1 else found[0]


def reorder_kernel(table_ref, in_ref, out_ref):
    count = table_ref.shape[0]
    size = in_ref.shape[1] // count
    for i in range(count):
        start = pl.multiple_of(table_ref[i] * size, size)
        out_ref[:, i * size : (i + 1) * size] = in_ref[:, pl.ds(start, size)]


def reorder(array, table):
    rows, width = array.shape
    block = min(128, rows)
    return pl.pallas_call(
        reorder_kernel,
        out_shape=jax.ShapeDtypeStruct(array.shape, array.dtype),
        grid_spec=pltpu.PrefetchScalarGridSpec(
            num_scalar_prefetch=1,
            grid=(rows // block,),
            in_specs=[pl.BlockSpec((block, width), lambda i, table: (i, 0))],
            out_specs=pl.BlockSpec((block, width), lambda i, table: (i, 0)),
        ),
        cost_estimate=pl.CostEstimate(
            flops=0, transcendentals=0, bytes_accessed=4 * rows * width
        ),
        name="reorder",
    )(table, array)


def norm_forward(values, gain, shift):
    average = jnp.mean(values, axis=-1, keepdims=True)
    centered = values - average
    inverse = lax.rsqrt(jnp.mean(centered * centered, axis=-1, keepdims=True) + EPSILON)
    unit = centered * inverse
    return unit * gain + shift, unit, inverse


def norm_backward(grad, unit, inverse, gain):
    scaled = grad * gain
    first = jnp.mean(scaled, axis=-1, keepdims=True)
    second = jnp.mean(scaled * unit, axis=-1, keepdims=True)
    terms = (jnp.sum(grad * unit, axis=0), jnp.sum(grad, axis=0))
    return (scaled - first - unit * second) * inverse, terms


def gelu_pair(values):
    root = 0.7978845608028654
    square = values * values
    inner = jnp.tanh(root * values * (1.0 + 0.044715 * square))
    half = 0.5 * (1.0 + inner)
    slope = half + 0.5 * values * (1.0 - inner * inner) * root * (1.0 + 3 * 0.044715 * square)
    return values * half, slope


def per_device(
    tokens,
    segments,
    query_weight,
    key_weight,
    value_weight,
    output_weight,
    expand_weight,
    contract_weight,
    norm_gains,
    norm_shifts,
    cotangent,
):
    dp_size = lax.axis_size("dp")
    tensor_size = lax.axis_size("tensor")
    halves = tokens.shape[0]
    tp = tensor_size // halves
    total = dp_size * tensor_size
    block_tokens, width = tokens.shape[1], tokens.shape[2]
    blocks = dp_size
    chips = dp_size // 2
    local_width = query_weight.shape[1]
    heads = local_width // DH
    core_bit, half_bit = tensor_size, tp
    t_bits = [1 << i for i in range(tp.bit_length() - 1)]
    p_bits = [1 << i for i in range(chips.bit_length() - 1)]
    orders = (p_bits, p_bits[::-1])
    dp_index, tensor_index = lax.axis_index("dp"), lax.axis_index("tensor")
    p, c = dp_index // 2, dp_index % 2
    h, t = tensor_index // tp, tensor_index % tp
    basis = (p * 2 + h).astype(jnp.int32)

    def reversed_bits(k):
        return sum(((k // bit) % 2) * (chips // 2 // bit) for bit in p_bits)

    def place(block):
        k, j = block // 2, block % 2
        return j * chips + jnp.where(j == 0, k, reversed_bits(k))

    numbers = jnp.arange(blocks, dtype=jnp.int32)
    rank = numbers % chips
    to_table = (
        jnp.where(numbers < chips, rank * 2, reversed_bits(rank) * 2 + 1).astype(jnp.int32) ^ basis
    )
    from_table = place(numbers ^ basis).astype(jnp.int32)
    home = c * tp + t

    def swap(array, mask):
        return lax.ppermute(array, AXES, [(i, i ^ mask) for i in range(total)])

    same = c == h

    def after(array, *others):
        return lax.optimization_barrier((array, *others))[0]


    def near(shard, other):
        got = swap(jnp.where(same, other, shard), core_bit)
        return [jnp.where(same, shard, got), jnp.where(same, got, other)]

    def moved(parts, step):
        got = [swap(v, order[step] * 2 * tensor_size) for v, order in zip(parts, orders)]
        return list(lax.optimization_barrier(tuple(got)))

    def joined(parts, got, axis):
        return [jnp.concatenate([v, w], axis=axis) for v, w in zip(parts, got)]

    def doubled(parts, axis, begin, end):
        for step in range(begin, end):
            parts = joined(parts, moved(parts, step), axis)
        return parts

    def tied(parts, *others):
        return list(lax.optimization_barrier((*parts, *others)))[: len(parts)]

    last = len(p_bits) - 1


    def split_send(parts, step, axis):
        halves_of = [jnp.split(v, 2, axis=axis) for v in parts]
        got = [
            swap(v[1], order[step] * 2 * tensor_size) for v, order in zip(halves_of, orders)
        ]
        return [v[0] for v in halves_of], list(lax.optimization_barrier(tuple(got)))

    def added(kept, got):
        return [(v.astype(F32) + w.astype(F32)).astype(BF16) for v, w in zip(kept, got)]

    def collect(first, second):
        got = swap(jnp.where(same, second, first), core_bit)
        kept = jnp.where(same, first, got)
        return kept, swap(jnp.where(same, got, second), half_bit)

    def reduce_rest(parts, axis, step):
        for s in range(step, -1, -1):
            parts = added(*split_send(parts, s, axis))
        kept, got = collect(*parts)
        return kept, got

    def total_of(kept, got):
        return kept.astype(F32) + got.astype(F32)


    def gather_far(array):
        parts = [array]
        for bit in t_bits:
            parts = parts + [swap(part, bit) for part in parts]
        return parts

    def gather_near(parts):
        return jnp.concatenate(parts + [swap(part, core_bit) for part in parts], axis=0)

    def gather_rows(array):
        return gather_near(gather_far(array))

    def reduce_near(array):
        array = array.astype(BF16)
        middle = array.shape[0] // 2
        return array[:middle].astype(F32) + swap(array[middle:], core_bit).astype(F32)

    def reduce_far(kept):
        for bit in t_bits[:0:-1]:
            middle = kept.shape[0] // 2
            kept = kept[:middle] + swap(kept[middle:].astype(BF16), bit).astype(F32)
        middle = kept.shape[0] // 2
        return kept[:middle], swap(kept[middle:].astype(BF16), t_bits[0])

    def ready(pair, *others):
        return pair[0] + after(pair[1], *others).astype(F32)

    own_segments = jnp.where(h == 0, segments[0, 0], segments[1, 0])
    other_segments = swap(own_segments, core_bit)

    def segments_of(j):
        row = jnp.where((h ^ j) == c, own_segments, other_segments)
        row = row.reshape(2 * tp, block_tokens)
        bits = [tp] + t_bits
        for bit in bits:
            moved = row.reshape(2 * tp // (2 * bit), 2, bit, block_tokens)
            moved = jnp.concatenate([moved[:, 1:], moved[:, :1]], axis=1)
            row = jnp.where((home & bit) != 0, moved.reshape(row.shape), row)
        row = row.reshape(-1)
        return row[:, None], row[None, :]

    def parted(array):
        return jnp.where(h == 0, array[0], array[1]), jnp.where(h == 0, array[1], array[0])

    def to_home(own, other):
        got = swap(jnp.where(same, other, own), core_bit)
        pair = [jnp.where(same, own, got), jnp.where(same, got, other)]
        both = reorder(jnp.concatenate(pair, axis=0), to_table)
        return [both[:block_tokens], both[block_tokens:]], both

    def sent_home(pieces):
        both = reorder(jnp.concatenate(pieces, axis=0), from_table)
        return collect(both[:block_tokens], both[block_tokens:])

    def home_pair(kept, got):
        return jnp.stack([jnp.where(h == 0, kept, got), jnp.where(h == 0, got, kept)])

    streams = range(2)
    extra = 16
    qkv_shard = jnp.stack(
        [w.reshape(-1, heads, DH) for w in (query_weight, key_weight, value_weight)], axis=2
    ).reshape(-1, 3 * local_width)
    params = jnp.concatenate([norm_gains, norm_shifts], axis=0)
    params = jnp.pad(params, ((0, extra - params.shape[0]), (0, 0)))
    output_shard = jnp.concatenate([output_weight, params], axis=0)

    qkv_other = swap(qkv_shard, half_bit)
    token_own, token_send = parted(tokens)
    token_other = swap(after(token_send, qkv_other), half_bit)
    qkv_parts = doubled(near(qkv_shard, qkv_other), 0, 0, 1)
    token_other = after(token_other, *qkv_parts)
    qkv_parts = tied(qkv_parts, token_other)
    output_other = swap(after(output_shard, token_other), half_bit)
    expand_other = swap(after(expand_weight, token_other), half_bit)
    homes, _ = to_home(token_own, token_other)
    sent = [gather_far(homes[0])]
    sent.append(gather_far(after(homes[1], *sent[0])))
    qkv_parts = doubled(qkv_parts, 0, 1, last)
    qkv_got = moved(qkv_parts, last)
    full_qkv = jnp.concatenate([qkv_parts[0], qkv_got[0], qkv_parts[1], qkv_got[1]], axis=0)
    output_other = after(output_other, full_qkv, sent[0][-1])
    output_parts = doubled(near(output_shard, output_other), 1, 0, last + 1)
    segs = [segments_of(j) for j in streams]

    rows = [gather_near(sent[0])]
    qkv = [dot_nn(rows[0], full_qkv).astype(BF16)]
    context = [attention_forward(qkv[0], *segs[0])]
    full_output = jnp.concatenate([x[:local_width] for x in output_parts], axis=1)
    params = jnp.concatenate([x[local_width : local_width + 4] for x in output_parts], axis=1)
    params = params.astype(F32)
    gains, shifts = params[:2], params[2:]
    partial = [reduce_near(dot_nn(context[0], full_output))]
    attended = [reduce_far(partial[0])]
    contract_other = swap(after(contract_weight, expand_other), half_bit)
    expand_parts = doubled(near(expand_weight, expand_other), 0, 0, last)
    sent1 = tied(sent[1], partial[0])
    pre = ()
    rows.append(after(gather_near(sent1), partial[0], *pre))
    qkv.append(dot_nn(rows[1], full_qkv).astype(BF16))
    pre = ()
    context.append(attention_forward(after(qkv[1], *pre), *segs[1]))
    expand_got = moved(tied(expand_parts, context[1]), last)

    pre = ()
    partial.append(reduce_near(dot_nn(after(context[1], *pre), full_output)))
    attended.append(reduce_far(partial[1]))
    attended[0] = ready(attended[0], partial[1])
    first = [norm_forward(homes[0].astype(F32) + attended[0], gains[0], shifts[0])]
    normed = [first[0][0].astype(BF16)]
    sent = [gather_far(normed[0])]
    contract_other = after(contract_other, context[1])
    pre = (contract_other, normed[0])
    first.append(
        norm_forward(homes[1].astype(F32) + ready(attended[1], *pre), gains[0], shifts[0])
    )
    normed.append(first[1][0].astype(BF16))
    sent.append(gather_far(normed[1]))
    cotangent_own, cotangent_send = parted(cotangent)
    cotangent_other = swap(after(cotangent_send, contract_other), half_bit)
    contract_parts = near(contract_weight, contract_other)
    expand_got = tied(expand_got, normed[1])
    full_expand = jnp.concatenate(
        [expand_parts[0], expand_got[0], expand_parts[1], expand_got[1]], axis=0
    )
    contract_parts = doubled(tied(contract_parts, *expand_got), 1, 0, last)
    normed_rows, active, slope, branch = [], [], [], []
    gate = tuple(contract_parts)
    contract_got = moved(contract_parts, last)

    def feed(j, *gate):
        normed_rows.append(after(gather_near(sent[j]), *gate))
        value, derivative = gelu_pair(dot_nn(normed_rows[j], full_expand))
        active.append(value.astype(BF16))
        slope.append(derivative.astype(BF16))

    feed(0, normed[1], *gate)
    feed(1, active[0])
    contract_got = tied(contract_got, active[1])
    full_contract = jnp.concatenate(
        [contract_parts[0], contract_got[0], contract_parts[1], contract_got[1]], axis=1
    )
    gate = active[1]
    branch.append(dot_nn(after(active[0], gate), full_contract).astype(BF16))
    partial = [reduce_near(branch[0])]
    pairs = [reduce_far(partial[0])]
    grads_home, grads_all = to_home(cotangent_own, after(cotangent_other, active[1]))
    gate = (branch[0],)
    branch.append(dot_nn(after(active[1], *gate), full_contract).astype(BF16))
    partial.append(reduce_near(branch[1]))
    pairs.append(reduce_far(partial[1]))

    second, branch_grad, sent = [], [], []
    gate = (partial[1], grads_all)
    for j in streams:
        second.append(norm_forward(first[j][0] + ready(pairs[j], *gate), gains[1], shifts[1]))
        branch_grad.append(
            norm_backward(grads_home[j].astype(F32), second[j][1], second[j][2], gains[1])
        )
        gate = (branch_grad[j][0].astype(BF16),)
        sent.append(gather_far(gate[0]))
    result_kept, result_got = sent_home([second[j][0].astype(BF16) for j in streams])
    branch_rows, hidden_grad, normed_part = [], [], []
    partial, pairs = [], []
    gate = (*gate, result_kept)
    for j in streams:
        branch_rows.append(after(gather_near(sent[j]), *gate))
        hidden_grad.append(
            (dot_nt(branch_rows[j], full_contract) * slope[j].astype(F32)).astype(BF16)
        )
        normed_part.append(dot_nt(hidden_grad[j], full_expand).astype(BF16))
        partial.append(reduce_near(normed_part[j]))
        pairs.append(reduce_far(partial[j]))
        if j == 0:
            branch_all = gather_near(sent[1])
            gate = partial[0]
            contract_grad = dot_tn(after(active[0], gate), branch_rows[0])
            contract_grad = contract_grad + dot_tn(active[1], branch_all)
            contract_grad = contract_grad.astype(BF16)
            result_got = after(result_got, partial[0])
            gate = (contract_grad,)
            gate = (*gate, result_got)
    contract_kept, contract_got = split_send(jnp.split(contract_grad, 2, axis=1), last, 1)
    result = home_pair(result_kept, result_got)
    normed_grad = [branch_grad[0][0] + ready(pairs[0], contract_grad)]
    first_grad = [norm_backward(normed_grad[0], first[0][1], first[0][2], gains[0])]
    gate = first_grad[0][0].astype(BF16)
    sent = [gather_far(gate)]
    expand_grad = dot_tn(after(normed_rows[0], gate, partial[1]), hidden_grad[0])
    contract_sum = added(contract_kept, tied(contract_got, partial[1]))
    pre = tuple(contract_sum)
    expand_grad = expand_grad + dot_tn(after(normed_rows[1], *pre), hidden_grad[1])
    expand_grad = expand_grad.astype(BF16)
    contract_kept, contract_got = split_send(contract_sum, last - 1, 1)
    expand_kept = jnp.split(expand_grad, 2, axis=0)
    expand_kept, expand_got = split_send(expand_kept, last, 0)
    normed_grad.append(branch_grad[1][0] + ready(pairs[1], expand_grad))
    first_grad.append(norm_backward(normed_grad[1], first[1][1], first[1][2], gains[0]))
    gate = first_grad[1][0].astype(BF16)
    sent.append(gather_far(gate))

    terms = jnp.stack(
        [
            sum(first_grad[j][1][0] for j in streams),
            sum(branch_grad[j][1][0] for j in streams),
            sum(first_grad[j][1][1] for j in streams),
            sum(branch_grad[j][1][1] for j in streams),
        ]
    )

    contract_sum = added(contract_kept, tied(contract_got, expand_grad))
    contract_kept, contract_got = reduce_rest(contract_sum, 1, last - 2)
    pre = (gate, contract_kept)
    attended_rows = [after(gather_near(sent[0]), expand_grad, *pre)]
    context_grad = dot_nt(attended_rows[0], full_output).astype(BF16)
    qkv_grad = [attention_backward(qkv[0], context_grad, *segs[0])]
    attended_rows.append(gather_near(tied(sent[1], qkv_grad[0])))
    expand_sum = added(expand_kept, tied(expand_got, qkv_grad[0]))
    expand_kept, expand_got = split_send(expand_sum, last - 1, 0)
    pre = tuple(expand_sum)
    tied_grad = after(qkv_grad[0], attended_rows[1], *pre)
    token_part = dot_nt(tied_grad, full_qkv).astype(BF16)
    partial = [reduce_near(token_part)]
    pairs = [reduce_far(partial[0])]
    terms = after(terms, attended_rows[1])
    for bit in t_bits + [core_bit]:
        terms = terms + swap(terms, bit)
    terms = jnp.pad(terms, ((0, extra - 4), (0, 0)))
    pre = ()
    output_grad = dot_tn(after(context[0], partial[0], *pre), attended_rows[0])
    output_grad = output_grad + dot_tn(context[1], attended_rows[1])
    output_grad = jnp.concatenate([output_grad, terms], axis=0).astype(BF16)
    output_kept, output_got = split_send(jnp.split(output_grad, 2, axis=1), last, 1)
    pre = ()
    context_grad = dot_nt(after(attended_rows[1], output_grad, *pre), full_output)
    qkv_grad.append(attention_backward(qkv[1], context_grad.astype(BF16), *segs[1]))
    expand_kept, expand_got = reduce_rest(
        added(expand_kept, tied(expand_got, qkv_grad[1])), 0, last - 2
    )
    output_sum = added(output_kept, tied(output_got, qkv_grad[1]))
    output_kept, output_got = split_send(output_sum, last - 1, 1)
    token_sums = [(first_grad[0][0] + ready(pairs[0], qkv_grad[1])).astype(BF16)]
    contract_got = after(contract_got, qkv_grad[1])
    pre = (contract_got,)
    pre = (*pre, token_sums[0])
    pre = (*pre, *output_sum)
    tied_grad = after(qkv_grad[1], expand_kept, *pre)
    token_part = dot_nt(tied_grad, full_qkv).astype(BF16)
    partial.append(reduce_near(token_part))
    pairs.append(reduce_far(partial[1]))
    middle = width // 2
    parts = []
    gate = (partial[1],)
    for i in range(2):
        columns = slice(i * middle, (i + 1) * middle)
        part = dot_tn(after(rows[0][:, columns], *gate), qkv_grad[0])
        parts.append((part + dot_tn(rows[1][:, columns], qkv_grad[1])).astype(BF16))
        if i == 0:
            gate = (parts[0],)
            expand_got = after(expand_got, parts[0])
            gate = (*gate, expand_got)
            output_got = tied(output_got, parts[0])
            output_kept, output_got = reduce_rest(added(output_kept, output_got), 1, last - 2)
            gate = (*gate, output_kept)
    pre = (parts[1],)
    token_sums.append((first_grad[1][0] + ready(pairs[1], *pre)).astype(BF16))
    tokens_kept, tokens_got = sent_home(token_sums)
    output_got = after(output_got, token_sums[1])
    output_grad = total_of(output_kept, output_got)
    tokens_grad = home_pair(tokens_kept, tokens_got).astype(F32)
    projection_grad = total_of(*reduce_rest(parts, 0, last))
    contract_grad = total_of(contract_kept, contract_got)
    expand_grad = total_of(expand_kept, expand_got)
    projection_grad = projection_grad.reshape(-1, heads, 3, DH)
    query_grad, key_grad, value_grad = [
        projection_grad[:, :, i].reshape(-1, local_width) for i in range(3)
    ]

    return (
        result,
        tokens_grad,
        query_grad,
        key_grad,
        value_grad,
        output_grad[:local_width],
        expand_grad,
        contract_grad,
        output_grad[local_width : local_width + 2],
        output_grad[local_width + 2 : local_width + 4],
    )


def solution(mesh):
    in_specs = (
        P(None, ("dp", "tensor"), None),
        P(None, "dp", None),
        P("dp", "tensor"),
        P("dp", "tensor"),
        P("dp", "tensor"),
        P("tensor", "dp"),
        P("dp", "tensor"),
        P("tensor", "dp"),
        P(None, "dp"),
        P(None, "dp"),
        P(None, ("dp", "tensor"), None),
    )
    out_specs = (
        P(None, ("dp", "tensor"), None),
        P(None, ("dp", "tensor"), None),
        P("dp", "tensor"),
        P("dp", "tensor"),
        P("dp", "tensor"),
        P("tensor", "dp"),
        P("dp", "tensor"),
        P("tensor", "dp"),
        P(None, "dp"),
        P(None, "dp"),
    )
    return jax.shard_map(
        per_device, mesh=mesh, in_specs=in_specs, out_specs=out_specs, check_vma=False
    )
```

```python
import functools

import jax
import jax.numpy as jnp
from jax import lax
from jax.experimental import pallas as pl
from jax.experimental.pallas import tpu as pltpu
from jax.sharding import PartitionSpec as P

DH = 128
EPSILON = 1e-06
NEGATIVE = -1e30
AXES = ("dp", "tensor")
HINT = 1 << 16
F32 = jnp.float32
BF16 = jnp.bfloat16


def dot_nn(left, right):
    return jnp.dot(left, right, preferred_element_type=F32)


def dot_tn(left, right):
    return lax.dot_general(left, right, (((0,), (0,)), ((), ())), preferred_element_type=F32)


def dot_nt(left, right):
    return lax.dot_general(left, right, (((1,), (1,)), ((), ())), preferred_element_type=F32)


def attention_forward_kernel(qkv_ref, seg_col_ref, seg_row_ref, out_ref, *, block):
    length = qkv_ref.shape[0]
    keys = qkv_ref[:, DH : 2 * DH]
    values = qkv_ref[:, 2 * DH :]
    seg_row = seg_row_ref[...]
    for start in range(0, length, block):
        rows = slice(start, start + block)
        scores = dot_nt(qkv_ref[rows, :DH], keys)
        scores = jnp.where(seg_col_ref[rows, :] == seg_row, scores, NEGATIVE)
        top = jnp.max(scores, axis=1, keepdims=True)
        exponent = jnp.exp((scores - top) * DH**-0.5)
        total = jnp.sum(exponent, axis=1, keepdims=True)
        context = dot_nn(exponent.astype(BF16), values)
        out_ref[rows, :] = (context / total).astype(BF16)


def attention_backward_kernel(
    qkv_ref, grad_ref, seg_col_ref, seg_row_ref, out_ref, key_total, value_total, *, block
):
    length = qkv_ref.shape[0]
    keys = qkv_ref[:, DH : 2 * DH]
    values = qkv_ref[:, 2 * DH :]
    seg_col = seg_col_ref[...]
    for start in range(0, length, block):
        rows = slice(start, start + block)
        query = qkv_ref[rows, :DH]
        grad = grad_ref[rows, :]
        scores = dot_nt(keys, query)
        scores = jnp.where(seg_col == seg_row_ref[:, rows], scores, NEGATIVE)
        top = jnp.max(scores, axis=0, keepdims=True)
        exponent = jnp.exp((scores - top) * DH**-0.5)
        probs = exponent * (1.0 / jnp.sum(exponent, axis=0, keepdims=True))
        prob_grad = dot_nt(values, grad)
        weighted = jnp.sum(probs * prob_grad, axis=0, keepdims=True)
        score_grad = (probs * (prob_grad - weighted)).astype(BF16)
        value_part = dot_nn(probs.astype(BF16), grad)
        key_part = dot_nn(score_grad, query)
        if start == 0:
            value_total[...] = value_part
            key_total[...] = key_part
        else:
            value_total[...] += value_part
            key_total[...] += key_part
        out_ref[rows, :DH] = (dot_tn(score_grad, keys) * DH**-0.5).astype(BF16)
    out_ref[:, DH : 2 * DH] = (key_total[...] * DH**-0.5).astype(BF16)
    out_ref[:, 2 * DH :] = value_total[...].astype(BF16)


def attention_forward(qkv, seg_col, seg_row):
    length, width = qkv.shape
    heads = width // (3 * DH)
    return pl.pallas_call(
        functools.partial(attention_forward_kernel, block=min(256, length)),
        out_shape=jax.ShapeDtypeStruct((length, heads * DH), BF16),
        grid=(heads,),
        in_specs=[
            pl.BlockSpec((length, 3 * DH), lambda i: (0, i)),
            pl.BlockSpec((length, 1), lambda i: (0, 0)),
            pl.BlockSpec((1, length), lambda i: (0, 0)),
        ],
        out_specs=pl.BlockSpec((length, DH), lambda i: (0, i)),
        cost_estimate=pl.CostEstimate(
            flops=HINT, transcendentals=0, bytes_accessed=HINT
        ),
        name="attention_forward",
    )(qkv, seg_col, seg_row)


def attention_backward(qkv, grad, seg_col, seg_row):
    length, width = qkv.shape
    heads = width // (3 * DH)
    return pl.pallas_call(
        functools.partial(attention_backward_kernel, block=min(256, length)),
        out_shape=jax.ShapeDtypeStruct((length, width), BF16),
        grid=(heads,),
        in_specs=[
            pl.BlockSpec((length, 3 * DH), lambda i: (0, i)),
            pl.BlockSpec((length, DH), lambda i: (0, i)),
            pl.BlockSpec((length, 1), lambda i: (0, 0)),
            pl.BlockSpec((1, length), lambda i: (0, 0)),
        ],
        out_specs=pl.BlockSpec((length, 3 * DH), lambda i: (0, i)),
        scratch_shapes=[pltpu.VMEM((length, DH), F32), pltpu.VMEM((length, DH), F32)],
        cost_estimate=pl.CostEstimate(
            flops=HINT, transcendentals=0, bytes_accessed=HINT
        ),
        name="attention_backward",
    )(qkv, grad, seg_col, seg_row)


def matmul_kernel(*refs, contract, finish, extras):
    left_ref, right_ref = refs[:2]
    product = lax.dot_general(
        left_ref[...], right_ref[...], (((1,), (contract,)), ((), ())), preferred_element_type=F32
    )
    results = finish(product, *[ref[...] for ref in refs[2 : 2 + extras]])
    for ref, value in zip(refs[2 + extras :], results):
        ref[...] = value.astype(ref.dtype)


def rounded(product):
    return (product,)


def matmul(left, right, transposed=False, finish=rounded, extras=(), outs=1, name="matmul"):
    rows, depth = left.shape
    columns = right.shape[0 if transposed else 1]
    block = min(512, columns)
    if transposed:
        right_spec = pl.BlockSpec((block, depth), lambda i: (i, 0))
    else:
        right_spec = pl.BlockSpec((depth, block), lambda i: (0, i))
    wide = pl.BlockSpec((rows, block), lambda i: (0, i))
    found = pl.pallas_call(
        functools.partial(
            matmul_kernel, contract=int(transposed), finish=finish, extras=len(extras)
        ),
        out_shape=[jax.ShapeDtypeStruct((rows, columns), BF16)] * outs,
        grid=(columns // block,),
        in_specs=[pl.BlockSpec((rows, depth), lambda i: (0, 0)), right_spec] + [wide] * len(extras),
        out_specs=[wide] * outs,
        cost_estimate=pl.CostEstimate(
            flops=HINT, transcendentals=0, bytes_accessed=HINT
        ),
        name=name,
    )(left, right, *extras)
    return found if outs > 1 else found[0]


def reorder_kernel(table_ref, in_ref, out_ref):
    count = table_ref.shape[0]
    size = in_ref.shape[1] // count
    for i in range(count):
        start = pl.multiple_of(table_ref[i] * size, size)
        out_ref[:, i * size : (i + 1) * size] = in_ref[:, pl.ds(start, size)]


def reorder(array, table):
    rows, width = array.shape
    block = min(128, rows)
    return pl.pallas_call(
        reorder_kernel,
        out_shape=jax.ShapeDtypeStruct(array.shape, array.dtype),
        grid_spec=pltpu.PrefetchScalarGridSpec(
            num_scalar_prefetch=1,
            grid=(rows // block,),
            in_specs=[pl.BlockSpec((block, width), lambda i, table: (i, 0))],
            out_specs=pl.BlockSpec((block, width), lambda i, table: (i, 0)),
        ),
        cost_estimate=pl.CostEstimate(
            flops=0, transcendentals=0, bytes_accessed=4 * rows * width
        ),
        name="reorder",
    )(table, array)


def norm_forward(values, gain, shift):
    average = jnp.mean(values, axis=-1, keepdims=True)
    centered = values - average
    inverse = lax.rsqrt(jnp.mean(centered * centered, axis=-1, keepdims=True) + EPSILON)
    unit = centered * inverse
    return unit * gain + shift, unit, inverse


def norm_backward(grad, unit, inverse, gain):
    scaled = grad * gain
    first = jnp.mean(scaled, axis=-1, keepdims=True)
    second = jnp.mean(scaled * unit, axis=-1, keepdims=True)
    terms = (jnp.sum(grad * unit, axis=0), jnp.sum(grad, axis=0))
    return (scaled - first - unit * second) * inverse, terms


def gelu_pair(values):
    root = 0.7978845608028654
    square = values * values
    inner = jnp.tanh(root * values * (1.0 + 0.044715 * square))
    half = 0.5 * (1.0 + inner)
    slope = half + 0.5 * values * (1.0 - inner * inner) * root * (1.0 + 3 * 0.044715 * square)
    return values * half, slope


def per_device(
    tokens,
    segments,
    query_weight,
    key_weight,
    value_weight,
    output_weight,
    expand_weight,
    contract_weight,
    norm_gains,
    norm_shifts,
    cotangent,
):
    dp_size = lax.axis_size("dp")
    tensor_size = lax.axis_size("tensor")
    halves = tokens.shape[0]
    tp = tensor_size // halves
    total = dp_size * tensor_size
    block_tokens, width = tokens.shape[1], tokens.shape[2]
    blocks = dp_size
    chips = dp_size // 2
    local_width = query_weight.shape[1]
    heads = local_width // DH
    core_bit, half_bit = tensor_size, tp
    t_bits = [1 << i for i in range(tp.bit_length() - 1)]
    p_bits = [1 << i for i in range(chips.bit_length() - 1)]
    orders = (p_bits, p_bits[::-1])
    dp_index, tensor_index = lax.axis_index("dp"), lax.axis_index("tensor")
    p, c = dp_index // 2, dp_index % 2
    h, t = tensor_index // tp, tensor_index % tp
    basis = (p * 2 + h).astype(jnp.int32)

    def reversed_bits(k):
        return sum(((k // bit) % 2) * (chips // 2 // bit) for bit in p_bits)

    def place(block):
        k, j = block // 2, block % 2
        return j * chips + jnp.where(j == 0, k, reversed_bits(k))

    numbers = jnp.arange(blocks, dtype=jnp.int32)
    rank = numbers % chips
    to_table = (
        jnp.where(numbers < chips, rank * 2, reversed_bits(rank) * 2 + 1).astype(jnp.int32) ^ basis
    )
    from_table = place(numbers ^ basis).astype(jnp.int32)
    home = c * tp + t

    def swap(array, mask):
        return lax.ppermute(array, AXES, [(i, i ^ mask) for i in range(total)])

    same = c == h

    def after(array, *others):
        return lax.optimization_barrier((array, *others))[0]


    def near(shard, other):
        got = swap(jnp.where(same, other, shard), core_bit)
        return [jnp.where(same, shard, got), jnp.where(same, got, other)]

    def moved(parts, step, pair=True):
        got = [swap(v, order[step] * 2 * tensor_size) for v, order in zip(parts, orders)]
        return list(lax.optimization_barrier(tuple(got))) if pair else got

    def joined(parts, got, axis):
        return [jnp.concatenate([v, w], axis=axis) for v, w in zip(parts, got)]

    def doubled(parts, axis, begin, end, pair=True):
        for step in range(begin, end):
            parts = joined(parts, moved(parts, step, pair), axis)
        return parts

    def tied(parts, *others):
        return list(lax.optimization_barrier((*parts, *others)))[: len(parts)]

    last = len(p_bits) - 1


    def split_send(parts, step, axis, pair=True):
        halves_of = [jnp.split(v, 2, axis=axis) for v in parts]
        got = [
            swap(v[1], order[step] * 2 * tensor_size) for v, order in zip(halves_of, orders)
        ]
        got = list(lax.optimization_barrier(tuple(got))) if pair else got
        return [v[0] for v in halves_of], got

    def added(kept, got):
        return [(v.astype(F32) + w.astype(F32)).astype(BF16) for v, w in zip(kept, got)]

    def collect(first, second):
        got = swap(jnp.where(same, second, first), core_bit)
        kept = jnp.where(same, first, got)
        return kept, swap(jnp.where(same, got, second), half_bit)

    def reduce_rest(parts, axis, step):
        for s in range(step, -1, -1):
            parts = added(*split_send(parts, s, axis))
        kept, got = collect(*parts)
        return kept, got

    def total_of(kept, got):
        return kept.astype(F32) + got.astype(F32)


    def gather_far(array):
        parts = [array]
        for bit in t_bits:
            parts = parts + [swap(part, bit) for part in parts]
        return parts

    def gather_near(parts):
        return jnp.concatenate(parts + [swap(part, core_bit) for part in parts], axis=0)

    def gather_rows(array):
        return gather_near(gather_far(array))

    def reduce_near(array):
        array = array.astype(BF16)
        middle = array.shape[0] // 2
        return array[:middle].astype(F32) + swap(array[middle:], core_bit).astype(F32)

    def reduce_far(kept):
        for bit in t_bits[:0:-1]:
            middle = kept.shape[0] // 2
            kept = kept[:middle] + swap(kept[middle:].astype(BF16), bit).astype(F32)
        middle = kept.shape[0] // 2
        return kept[:middle], swap(kept[middle:].astype(BF16), t_bits[0])

    def ready(pair, *others):
        return pair[0] + after(pair[1], *others).astype(F32)

    own_segments = jnp.where(h == 0, segments[0, 0], segments[1, 0])
    other_segments = swap(own_segments, core_bit)

    def segments_of(j):
        row = jnp.where((h ^ j) == c, own_segments, other_segments)
        row = row.reshape(2 * tp, block_tokens)
        bits = [tp] + t_bits
        for bit in bits:
            moved = row.reshape(2 * tp // (2 * bit), 2, bit, block_tokens)
            moved = jnp.concatenate([moved[:, 1:], moved[:, :1]], axis=1)
            row = jnp.where((home & bit) != 0, moved.reshape(row.shape), row)
        row = row.reshape(-1)
        return row[:, None], row[None, :]

    def parted(array):
        return jnp.where(h == 0, array[0], array[1]), jnp.where(h == 0, array[1], array[0])

    def to_home(own, other):
        got = swap(jnp.where(same, other, own), core_bit)
        pair = [jnp.where(same, own, got), jnp.where(same, got, other)]
        both = reorder(jnp.concatenate(pair, axis=0), to_table)
        return [both[:block_tokens], both[block_tokens:]], both

    def sent_home(pieces):
        both = reorder(jnp.concatenate(pieces, axis=0), from_table)
        return collect(both[:block_tokens], both[block_tokens:])

    def home_pair(kept, got):
        return jnp.stack([jnp.where(h == 0, kept, got), jnp.where(h == 0, got, kept)])

    streams = range(2)
    pair_q = False
    pair_o = True
    pair_e = True
    pair_c = False
    send_c = True
    send_e = False
    send_o = False
    extra = 16
    qkv_shard = jnp.stack(
        [w.reshape(-1, heads, DH) for w in (query_weight, key_weight, value_weight)], axis=2
    ).reshape(-1, 3 * local_width)
    params = jnp.concatenate([norm_gains, norm_shifts], axis=0)
    params = jnp.pad(params, ((0, extra - params.shape[0]), (0, 0)))
    output_shard = jnp.concatenate([output_weight, params], axis=0)

    qkv_other = swap(qkv_shard, half_bit)
    token_own, token_send = parted(tokens)
    token_other = swap(after(token_send, qkv_other), half_bit)
    qkv_parts = doubled(near(qkv_shard, qkv_other), 0, 0, 1, pair_q)
    token_other = after(token_other, *qkv_parts)
    qkv_parts = tied(qkv_parts, token_other)
    output_other = swap(after(output_shard, token_other), half_bit)
    expand_other = swap(after(expand_weight, token_other), half_bit)
    homes, _ = to_home(token_own, token_other)
    sent = [gather_far(homes[0])]
    sent.append(gather_far(after(homes[1], *sent[0])))
    qkv_parts = doubled(qkv_parts, 0, 1, last, pair_q)
    qkv_got = moved(qkv_parts, last, pair_q)
    full_qkv = jnp.concatenate([qkv_parts[0], qkv_got[0], qkv_parts[1], qkv_got[1]], axis=0)
    output_other = after(output_other, full_qkv, sent[0][-1])
    output_parts = doubled(near(output_shard, output_other), 1, 0, last + 1, pair_o)
    segs = [segments_of(j) for j in streams]

    rows = [gather_near(sent[0])]
    qkv = [dot_nn(rows[0], full_qkv).astype(BF16)]
    context = [attention_forward(qkv[0], *segs[0])]
    full_output = jnp.concatenate([x[:local_width] for x in output_parts], axis=1)
    params = jnp.concatenate([x[local_width : local_width + 4] for x in output_parts], axis=1)
    params = params.astype(F32)
    gains, shifts = params[:2], params[2:]
    partial = [reduce_near(dot_nn(context[0], full_output))]
    attended = [reduce_far(partial[0])]
    contract_other = swap(after(contract_weight, expand_other), half_bit)
    expand_other = after(expand_other, context[0])
    expand_parts = doubled(near(expand_weight, expand_other), 0, 0, last, pair_e)
    sent1 = tied(sent[1], context[0])
    pre = ()
    rows.append(after(gather_near(sent1), partial[0], *pre))
    qkv.append(dot_nn(rows[1], full_qkv).astype(BF16))
    pre = ()
    context.append(attention_forward(after(qkv[1], *pre), *segs[1]))
    expand_got = moved(tied(expand_parts, context[1]), last, pair_e)

    pre = ()
    partial.append(reduce_near(dot_nn(after(context[1], *pre), full_output)))
    attended.append(reduce_far(partial[1]))
    attended[0] = ready(attended[0], partial[1])
    first = [norm_forward(homes[0].astype(F32) + attended[0], gains[0], shifts[0])]
    normed = [first[0][0].astype(BF16)]
    sent = [gather_far(normed[0])]
    contract_other = after(contract_other, context[1])
    pre = (normed[0],)
    first.append(
        norm_forward(homes[1].astype(F32) + ready(attended[1], *pre), gains[0], shifts[0])
    )
    normed.append(first[1][0].astype(BF16))
    sent.append(gather_far(normed[1]))
    cotangent_own, cotangent_send = parted(cotangent)
    contract_parts = near(contract_weight, contract_other)
    expand_got = tied(expand_got, normed[1])
    full_expand = jnp.concatenate(
        [expand_parts[0], expand_got[0], expand_parts[1], expand_got[1]], axis=0
    )
    contract_parts = doubled(tied(contract_parts, *expand_got), 1, 0, last, pair_c)
    normed_rows, active, slope, branch = [], [], [], []
    gate = tuple(contract_parts)
    contract_got = moved(contract_parts, last, pair_c)

    def feed(j, *gate):
        normed_rows.append(after(gather_near(sent[j]), *gate))
        value, derivative = gelu_pair(dot_nn(normed_rows[j], full_expand))
        active.append(value.astype(BF16))
        slope.append(derivative.astype(BF16))

    feed(0, normed[1], *gate)
    cotangent_other = swap(after(cotangent_send, contract_other, active[0]), half_bit)
    feed(1, active[0])
    contract_got = tied(contract_got, active[1])
    full_contract = jnp.concatenate(
        [contract_parts[0], contract_got[0], contract_parts[1], contract_got[1]], axis=1
    )
    gate = active[1]
    branch.append(dot_nn(after(active[0], gate), full_contract).astype(BF16))
    partial = [reduce_near(branch[0])]
    pairs = [reduce_far(partial[0])]
    grads_home, grads_all = to_home(cotangent_own, cotangent_other)
    gate = (branch[0],)
    branch.append(dot_nn(after(active[1], *gate), full_contract).astype(BF16))
    partial.append(reduce_near(branch[1]))
    pairs.append(reduce_far(partial[1]))

    second, branch_grad, sent = [], [], []
    gate = (branch[1], grads_all)
    for j in streams:
        second.append(norm_forward(first[j][0] + ready(pairs[j], *gate), gains[1], shifts[1]))
        branch_grad.append(
            norm_backward(grads_home[j].astype(F32), second[j][1], second[j][2], gains[1])
        )
        gate = (branch_grad[j][0].astype(BF16),)
        sent.append(gather_far(gate[0]))
        if j == 0:
            gate = ()
    result_kept, result_got = sent_home([second[j][0].astype(BF16) for j in streams])
    branch_rows, hidden_grad, normed_part = [], [], []
    partial, pairs = [], []
    gate = (*gate, result_kept)
    for j in streams:
        branch_rows.append(after(gather_near(sent[j]), *gate))
        hidden_grad.append(
            (dot_nt(branch_rows[j], full_contract) * slope[j].astype(F32)).astype(BF16)
        )
        normed_part.append(dot_nt(hidden_grad[j], full_expand).astype(BF16))
        partial.append(reduce_near(normed_part[j]))
        pairs.append(reduce_far(partial[j]))
        if j == 0:
            branch_all = gather_near(sent[1])
            gate = partial[0]
            contract_grad = dot_tn(after(active[0], gate), branch_rows[0])
            contract_grad = contract_grad + dot_tn(active[1], branch_all)
            contract_grad = contract_grad.astype(BF16)
            result_got = after(result_got, partial[0])
            gate = (contract_grad,)
            gate = (*gate, result_got)
    contract_kept, contract_got = split_send(jnp.split(contract_grad, 2, axis=1), last, 1, send_c)
    result = home_pair(result_kept, result_got)
    normed_grad = [branch_grad[0][0] + ready(pairs[0], contract_grad)]
    first_grad = [norm_backward(normed_grad[0], first[0][1], first[0][2], gains[0])]
    gate = first_grad[0][0].astype(BF16)
    sent = [gather_far(gate)]
    expand_grad = dot_tn(after(normed_rows[0], gate, normed_part[1]), hidden_grad[0])
    contract_sum = added(contract_kept, tied(contract_got, partial[1]))
    pre = tuple(contract_sum)
    expand_grad = expand_grad + dot_tn(after(normed_rows[1], *pre), hidden_grad[1])
    expand_grad = expand_grad.astype(BF16)
    contract_kept, contract_got = split_send(contract_sum, last - 1, 1, send_c)
    expand_kept = jnp.split(expand_grad, 2, axis=0)
    expand_kept, expand_got = split_send(expand_kept, last, 0, send_e)
    normed_grad.append(branch_grad[1][0] + ready(pairs[1], expand_grad))
    first_grad.append(norm_backward(normed_grad[1], first[1][1], first[1][2], gains[0]))
    gate = first_grad[1][0].astype(BF16)
    sent.append(gather_far(gate))

    terms = jnp.stack(
        [
            sum(first_grad[j][1][0] for j in streams),
            sum(branch_grad[j][1][0] for j in streams),
            sum(first_grad[j][1][1] for j in streams),
            sum(branch_grad[j][1][1] for j in streams),
        ]
    )

    contract_sum = added(contract_kept, tied(contract_got, expand_grad))
    contract_kept, contract_got = reduce_rest(contract_sum, 1, last - 2)
    pre = (gate, contract_kept)
    attended_rows = [after(gather_near(sent[0]), expand_grad, *pre)]
    context_grad = dot_nt(attended_rows[0], full_output).astype(BF16)
    qkv_grad = [attention_backward(qkv[0], context_grad, *segs[0])]
    attended_rows.append(gather_near(tied(sent[1], qkv_grad[0])))
    expand_sum = added(expand_kept, tied(expand_got, qkv_grad[0]))
    expand_kept, expand_got = split_send(expand_sum, last - 1, 0, send_e)
    pre = tuple(expand_sum)
    tied_grad = after(qkv_grad[0], attended_rows[1], *pre)
    token_part = dot_nt(tied_grad, full_qkv).astype(BF16)
    partial = [reduce_near(token_part)]
    pairs = [reduce_far(partial[0])]
    terms = after(terms, attended_rows[1])
    for bit in t_bits + [core_bit]:
        terms = terms + swap(terms, bit)
    terms = jnp.pad(terms, ((0, extra - 4), (0, 0)))
    pre = ()
    output_grad = dot_tn(after(context[0], partial[0], *pre), attended_rows[0])
    output_grad = output_grad + dot_tn(context[1], attended_rows[1])
    output_grad = jnp.concatenate([output_grad, terms], axis=0).astype(BF16)
    output_kept, output_got = split_send(jnp.split(output_grad, 2, axis=1), last, 1, send_o)
    pre = ()
    context_grad = dot_nt(after(attended_rows[1], output_grad, *pre), full_output)
    qkv_grad.append(attention_backward(qkv[1], context_grad.astype(BF16), *segs[1]))
    expand_kept, expand_got = reduce_rest(
        added(expand_kept, tied(expand_got, qkv_grad[1])), 0, last - 2
    )
    output_sum = added(output_kept, tied(output_got, qkv_grad[1]))
    output_kept, output_got = split_send(output_sum, last - 1, 1, send_o)
    token_sums = [(first_grad[0][0] + ready(pairs[0], qkv_grad[1])).astype(BF16)]
    contract_got = after(contract_got, qkv_grad[1])
    pre = (contract_got,)
    pre = (*pre, token_sums[0])
    pre = (*pre, *output_sum)
    tied_grad = after(qkv_grad[1], expand_kept, *pre)
    token_part = dot_nt(tied_grad, full_qkv).astype(BF16)
    partial.append(reduce_near(token_part))
    pairs.append(reduce_far(partial[1]))
    middle = width // 2
    parts = []
    gate = (partial[1],)
    for i in range(2):
        columns = slice(i * middle, (i + 1) * middle)
        part = dot_tn(after(rows[0][:, columns], *gate), qkv_grad[0])
        parts.append((part + dot_tn(rows[1][:, columns], qkv_grad[1])).astype(BF16))
        if i == 0:
            gate = (parts[0],)
    expand_got = after(expand_got, parts[1])
    pre = (parts[1], expand_got)
    token_sums.append((first_grad[1][0] + ready(pairs[1], *pre)).astype(BF16))
    tokens_kept, tokens_got = sent_home(token_sums)
    output_kept, output_got = reduce_rest(added(output_kept, output_got), 1, last - 2)
    output_got = after(output_got, token_sums[1])
    output_grad = total_of(output_kept, output_got)
    tokens_grad = home_pair(tokens_kept, tokens_got).astype(F32)
    projection_grad = total_of(*reduce_rest(parts, 0, last))
    contract_grad = total_of(contract_kept, contract_got)
    expand_grad = total_of(expand_kept, expand_got)
    projection_grad = projection_grad.reshape(-1, heads, 3, DH)
    query_grad, key_grad, value_grad = [
        projection_grad[:, :, i].reshape(-1, local_width) for i in range(3)
    ]

    return (
        result,
        tokens_grad,
        query_grad,
        key_grad,
        value_grad,
        output_grad[:local_width],
        expand_grad,
        contract_grad,
        output_grad[local_width : local_width + 2],
        output_grad[local_width + 2 : local_width + 4],
    )


def solution(mesh):
    in_specs = (
        P(None, ("dp", "tensor"), None),
        P(None, "dp", None),
        P("dp", "tensor"),
        P("dp", "tensor"),
        P("dp", "tensor"),
        P("tensor", "dp"),
        P("dp", "tensor"),
        P("tensor", "dp"),
        P(None, "dp"),
        P(None, "dp"),
        P(None, ("dp", "tensor"), None),
    )
    out_specs = (
        P(None, ("dp", "tensor"), None),
        P(None, ("dp", "tensor"), None),
        P("dp", "tensor"),
        P("dp", "tensor"),
        P("dp", "tensor"),
        P("tensor", "dp"),
        P("dp", "tensor"),
        P("tensor", "dp"),
        P(None, "dp"),
        P(None, "dp"),
    )
    return jax.shard_map(
        per_device, mesh=mesh, in_specs=in_specs, out_specs=out_specs, check_vma=False
    )
```

```python
import functools

import jax
import jax.numpy as jnp
from jax import lax
from jax.experimental import pallas as pl
from jax.experimental.pallas import tpu as pltpu
from jax.sharding import PartitionSpec as P

DH = 128
EPSILON = 1e-06
NEGATIVE = -1e30
AXES = ("dp", "tensor")
HINT = 1 << 16
F32 = jnp.float32
BF16 = jnp.bfloat16


def dot_nn(left, right):
    return jnp.dot(left, right, preferred_element_type=F32)


def dot_tn(left, right):
    return lax.dot_general(left, right, (((0,), (0,)), ((), ())), preferred_element_type=F32)


def dot_nt(left, right):
    return lax.dot_general(left, right, (((1,), (1,)), ((), ())), preferred_element_type=F32)


def attention_forward_kernel(qkv_ref, seg_col_ref, seg_row_ref, out_ref, *, block):
    length = qkv_ref.shape[0]
    keys = qkv_ref[:, DH : 2 * DH]
    values = qkv_ref[:, 2 * DH :]
    seg_row = seg_row_ref[...]
    for start in range(0, length, block):
        rows = slice(start, start + block)
        scores = dot_nt(qkv_ref[rows, :DH], keys)
        scores = jnp.where(seg_col_ref[rows, :] == seg_row, scores, NEGATIVE)
        top = jnp.max(scores, axis=1, keepdims=True)
        exponent = jnp.exp((scores - top) * DH**-0.5)
        total = jnp.sum(exponent, axis=1, keepdims=True)
        context = dot_nn(exponent.astype(BF16), values)
        out_ref[rows, :] = (context / total).astype(BF16)


def attention_backward_kernel(
    qkv_ref, grad_ref, seg_col_ref, seg_row_ref, out_ref, key_total, value_total, *, block
):
    length = qkv_ref.shape[0]
    keys = qkv_ref[:, DH : 2 * DH]
    values = qkv_ref[:, 2 * DH :]
    seg_col = seg_col_ref[...]
    for start in range(0, length, block):
        rows = slice(start, start + block)
        query = qkv_ref[rows, :DH]
        grad = grad_ref[rows, :]
        scores = dot_nt(keys, query)
        scores = jnp.where(seg_col == seg_row_ref[:, rows], scores, NEGATIVE)
        top = jnp.max(scores, axis=0, keepdims=True)
        exponent = jnp.exp((scores - top) * DH**-0.5)
        probs = exponent * (1.0 / jnp.sum(exponent, axis=0, keepdims=True))
        prob_grad = dot_nt(values, grad)
        weighted = jnp.sum(probs * prob_grad, axis=0, keepdims=True)
        score_grad = (probs * (prob_grad - weighted)).astype(BF16)
        value_part = dot_nn(probs.astype(BF16), grad)
        key_part = dot_nn(score_grad, query)
        if start == 0:
            value_total[...] = value_part
            key_total[...] = key_part
        else:
            value_total[...] += value_part
            key_total[...] += key_part
        out_ref[rows, :DH] = (dot_tn(score_grad, keys) * DH**-0.5).astype(BF16)
    out_ref[:, DH : 2 * DH] = (key_total[...] * DH**-0.5).astype(BF16)
    out_ref[:, 2 * DH :] = value_total[...].astype(BF16)


def attention_forward(qkv, seg_col, seg_row):
    length, width = qkv.shape
    heads = width // (3 * DH)
    return pl.pallas_call(
        functools.partial(attention_forward_kernel, block=min(256, length)),
        out_shape=jax.ShapeDtypeStruct((length, heads * DH), BF16),
        grid=(heads,),
        in_specs=[
            pl.BlockSpec((length, 3 * DH), lambda i: (0, i)),
            pl.BlockSpec((length, 1), lambda i: (0, 0)),
            pl.BlockSpec((1, length), lambda i: (0, 0)),
        ],
        out_specs=pl.BlockSpec((length, DH), lambda i: (0, i)),
        cost_estimate=pl.CostEstimate(
            flops=HINT, transcendentals=0, bytes_accessed=HINT
        ),
        name="attention_forward",
    )(qkv, seg_col, seg_row)


def attention_backward(qkv, grad, seg_col, seg_row):
    length, width = qkv.shape
    heads = width // (3 * DH)
    return pl.pallas_call(
        functools.partial(attention_backward_kernel, block=min(256, length)),
        out_shape=jax.ShapeDtypeStruct((length, width), BF16),
        grid=(heads,),
        in_specs=[
            pl.BlockSpec((length, 3 * DH), lambda i: (0, i)),
            pl.BlockSpec((length, DH), lambda i: (0, i)),
            pl.BlockSpec((length, 1), lambda i: (0, 0)),
            pl.BlockSpec((1, length), lambda i: (0, 0)),
        ],
        out_specs=pl.BlockSpec((length, 3 * DH), lambda i: (0, i)),
        scratch_shapes=[pltpu.VMEM((length, DH), F32), pltpu.VMEM((length, DH), F32)],
        cost_estimate=pl.CostEstimate(
            flops=HINT, transcendentals=0, bytes_accessed=HINT
        ),
        name="attention_backward",
    )(qkv, grad, seg_col, seg_row)


def matmul_kernel(*refs, contract, finish, extras):
    left_ref, right_ref = refs[:2]
    product = lax.dot_general(
        left_ref[...], right_ref[...], (((1,), (contract,)), ((), ())), preferred_element_type=F32
    )
    results = finish(product, *[ref[...] for ref in refs[2 : 2 + extras]])
    for ref, value in zip(refs[2 + extras :], results):
        ref[...] = value.astype(ref.dtype)


def rounded(product):
    return (product,)


def matmul(left, right, transposed=False, finish=rounded, extras=(), outs=1, name="matmul"):
    rows, depth = left.shape
    columns = right.shape[0 if transposed else 1]
    block = min(512, columns)
    if transposed:
        right_spec = pl.BlockSpec((block, depth), lambda i: (i, 0))
    else:
        right_spec = pl.BlockSpec((depth, block), lambda i: (0, i))
    wide = pl.BlockSpec((rows, block), lambda i: (0, i))
    found = pl.pallas_call(
        functools.partial(
            matmul_kernel, contract=int(transposed), finish=finish, extras=len(extras)
        ),
        out_shape=[jax.ShapeDtypeStruct((rows, columns), BF16)] * outs,
        grid=(columns // block,),
        in_specs=[pl.BlockSpec((rows, depth), lambda i: (0, 0)), right_spec] + [wide] * len(extras),
        out_specs=[wide] * outs,
        cost_estimate=pl.CostEstimate(
            flops=HINT, transcendentals=0, bytes_accessed=HINT
        ),
        name=name,
    )(left, right, *extras)
    return found if outs > 1 else found[0]


def reorder_kernel(table_ref, in_ref, out_ref):
    count = table_ref.shape[0]
    size = in_ref.shape[1] // count
    for i in range(count):
        start = pl.multiple_of(table_ref[i] * size, size)
        out_ref[:, i * size : (i + 1) * size] = in_ref[:, pl.ds(start, size)]


def reorder(array, table):
    rows, width = array.shape
    block = min(128, rows)
    return pl.pallas_call(
        reorder_kernel,
        out_shape=jax.ShapeDtypeStruct(array.shape, array.dtype),
        grid_spec=pltpu.PrefetchScalarGridSpec(
            num_scalar_prefetch=1,
            grid=(rows // block,),
            in_specs=[pl.BlockSpec((block, width), lambda i, table: (i, 0))],
            out_specs=pl.BlockSpec((block, width), lambda i, table: (i, 0)),
        ),
        cost_estimate=pl.CostEstimate(
            flops=0, transcendentals=0, bytes_accessed=4 * rows * width
        ),
        name="reorder",
    )(table, array)


def norm_forward(values, gain, shift):
    average = jnp.mean(values, axis=-1, keepdims=True)
    centered = values - average
    inverse = lax.rsqrt(jnp.mean(centered * centered, axis=-1, keepdims=True) + EPSILON)
    unit = centered * inverse
    return unit * gain + shift, unit, inverse


def norm_backward(grad, unit, inverse, gain):
    scaled = grad * gain
    first = jnp.mean(scaled, axis=-1, keepdims=True)
    second = jnp.mean(scaled * unit, axis=-1, keepdims=True)
    terms = (jnp.sum(grad * unit, axis=0), jnp.sum(grad, axis=0))
    return (scaled - first - unit * second) * inverse, terms


def gelu_pair(values):
    root = 0.7978845608028654
    square = values * values
    inner = jnp.tanh(root * values * (1.0 + 0.044715 * square))
    half = 0.5 * (1.0 + inner)
    slope = half + 0.5 * values * (1.0 - inner * inner) * root * (1.0 + 3 * 0.044715 * square)
    return values * half, slope


def per_device(
    tokens,
    segments,
    query_weight,
    key_weight,
    value_weight,
    output_weight,
    expand_weight,
    contract_weight,
    norm_gains,
    norm_shifts,
    cotangent,
):
    dp_size = lax.axis_size("dp")
    tensor_size = lax.axis_size("tensor")
    halves = tokens.shape[0]
    tp = tensor_size // halves
    total = dp_size * tensor_size
    block_tokens, width = tokens.shape[1], tokens.shape[2]
    blocks = dp_size
    chips = dp_size // 2
    local_width = query_weight.shape[1]
    heads = local_width // DH
    core_bit, half_bit = tensor_size, tp
    t_bits = [1 << i for i in range(tp.bit_length() - 1)]
    p_bits = [1 << i for i in range(chips.bit_length() - 1)]
    orders = (p_bits, p_bits[::-1])
    dp_index, tensor_index = lax.axis_index("dp"), lax.axis_index("tensor")
    p, c = dp_index // 2, dp_index % 2
    h, t = tensor_index // tp, tensor_index % tp
    basis = (p * 2 + h).astype(jnp.int32)

    def reversed_bits(k):
        return sum(((k // bit) % 2) * (chips // 2 // bit) for bit in p_bits)

    def place(block):
        k, j = block // 2, block % 2
        return j * chips + jnp.where(j == 0, k, reversed_bits(k))

    numbers = jnp.arange(blocks, dtype=jnp.int32)
    rank = numbers % chips
    to_table = (
        jnp.where(numbers < chips, rank * 2, reversed_bits(rank) * 2 + 1).astype(jnp.int32) ^ basis
    )
    from_table = place(numbers ^ basis).astype(jnp.int32)
    home = c * tp + t

    def swap(array, mask):
        return lax.ppermute(array, AXES, [(i, i ^ mask) for i in range(total)])

    same = c == h

    def after(array, *others):
        return lax.optimization_barrier((array, *others))[0]


    def near(shard, other):
        got = swap(jnp.where(same, other, shard), core_bit)
        return [jnp.where(same, shard, got), jnp.where(same, got, other)]

    def moved(parts, step, pair=True):
        got = [swap(v, order[step] * 2 * tensor_size) for v, order in zip(parts, orders)]
        return list(lax.optimization_barrier(tuple(got))) if pair else got

    def joined(parts, got, axis):
        return [jnp.concatenate([v, w], axis=axis) for v, w in zip(parts, got)]

    def doubled(parts, axis, begin, end, pair=True):
        for step in range(begin, end):
            parts = joined(parts, moved(parts, step, pair), axis)
        return parts

    def tied(parts, *others):
        return list(lax.optimization_barrier((*parts, *others)))[: len(parts)]

    last = len(p_bits) - 1


    def split_send(parts, step, axis, pair=True):
        halves_of = [jnp.split(v, 2, axis=axis) for v in parts]
        got = [
            swap(v[1], order[step] * 2 * tensor_size) for v, order in zip(halves_of, orders)
        ]
        got = list(lax.optimization_barrier(tuple(got))) if pair else got
        return [v[0] for v in halves_of], got

    def added(kept, got):
        return [(v.astype(F32) + w.astype(F32)).astype(BF16) for v, w in zip(kept, got)]

    def collect(first, second):
        got = swap(jnp.where(same, second, first), core_bit)
        kept = jnp.where(same, first, got)
        return kept, swap(jnp.where(same, got, second), half_bit)

    def reduce_rest(parts, axis, step):
        for s in range(step, -1, -1):
            parts = added(*split_send(parts, s, axis))
        kept, got = collect(*parts)
        return kept, got

    def total_of(kept, got):
        return kept.astype(F32) + got.astype(F32)


    def gather_far(array):
        parts = [array]
        for bit in t_bits:
            parts = parts + [swap(part, bit) for part in parts]
        return parts

    def gather_near(parts):
        return jnp.concatenate(parts + [swap(part, core_bit) for part in parts], axis=0)

    def gather_rows(array):
        return gather_near(gather_far(array))

    def reduce_near(array):
        array = array.astype(BF16)
        middle = array.shape[0] // 2
        return array[:middle].astype(F32) + swap(array[middle:], core_bit).astype(F32)

    def reduce_far(kept):
        for bit in t_bits[:0:-1]:
            middle = kept.shape[0] // 2
            kept = kept[:middle] + swap(kept[middle:].astype(BF16), bit).astype(F32)
        middle = kept.shape[0] // 2
        return kept[:middle], swap(kept[middle:].astype(BF16), t_bits[0])

    def ready(pair, *others):
        return pair[0] + after(pair[1], *others).astype(F32)

    own_segments = jnp.where(h == 0, segments[0, 0], segments[1, 0])
    other_segments = swap(own_segments, core_bit)

    def segments_of(j):
        row = jnp.where((h ^ j) == c, own_segments, other_segments)
        row = row.reshape(2 * tp, block_tokens)
        bits = [tp] + t_bits
        for bit in bits:
            moved = row.reshape(2 * tp // (2 * bit), 2, bit, block_tokens)
            moved = jnp.concatenate([moved[:, 1:], moved[:, :1]], axis=1)
            row = jnp.where((home & bit) != 0, moved.reshape(row.shape), row)
        row = row.reshape(-1)
        return row[:, None], row[None, :]

    def parted(array):
        return jnp.where(h == 0, array[0], array[1]), jnp.where(h == 0, array[1], array[0])

    def to_home(own, other):
        got = swap(jnp.where(same, other, own), core_bit)
        pair = [jnp.where(same, own, got), jnp.where(same, got, other)]
        both = reorder(jnp.concatenate(pair, axis=0), to_table)
        return [both[:block_tokens], both[block_tokens:]], both

    def sent_home(pieces):
        both = reorder(jnp.concatenate(pieces, axis=0), from_table)
        return collect(both[:block_tokens], both[block_tokens:])

    def home_pair(kept, got):
        return jnp.stack([jnp.where(h == 0, kept, got), jnp.where(h == 0, got, kept)])

    streams = range(2)
    pair_q = False
    pair_o = True
    pair_e = False
    pair_c = False
    send_c = True
    send_e = False
    send_o = False
    extra = 16
    qkv_shard = jnp.stack(
        [w.reshape(-1, heads, DH) for w in (query_weight, key_weight, value_weight)], axis=2
    ).reshape(-1, 3 * local_width)
    params = jnp.concatenate([norm_gains, norm_shifts], axis=0)
    params = jnp.pad(params, ((0, extra - params.shape[0]), (0, 0)))
    output_shard = jnp.concatenate([output_weight, params], axis=0)

    qkv_other = swap(qkv_shard, half_bit)
    token_own, token_send = parted(tokens)
    token_other = swap(after(token_send, qkv_other), half_bit)
    qkv_parts = doubled(near(qkv_shard, qkv_other), 0, 0, 1, pair_q)
    token_other = after(token_other, *qkv_parts)
    qkv_parts = tied(qkv_parts, token_other)
    output_other = swap(after(output_shard, token_other), half_bit)
    expand_other = swap(after(expand_weight, token_other), half_bit)
    homes, _ = to_home(token_own, token_other)
    sent = [gather_far(homes[0])]
    sent.append(gather_far(homes[1]))
    qkv_parts = doubled(qkv_parts, 0, 1, last, pair_q)
    qkv_got = moved(qkv_parts, last, pair_q)
    full_qkv = jnp.concatenate([qkv_parts[0], qkv_got[0], qkv_parts[1], qkv_got[1]], axis=0)
    output_other = after(output_other, full_qkv, sent[0][-1])
    output_parts = doubled(near(output_shard, output_other), 1, 0, last + 1, pair_o)
    segs = [segments_of(j) for j in streams]

    rows = [gather_near(sent[0])]
    qkv = [dot_nn(rows[0], full_qkv).astype(BF16)]
    context = [attention_forward(qkv[0], *segs[0])]
    full_output = jnp.concatenate([x[:local_width] for x in output_parts], axis=1)
    params = jnp.concatenate([x[local_width : local_width + 4] for x in output_parts], axis=1)
    params = params.astype(F32)
    gains, shifts = params[:2], params[2:]
    partial = [reduce_near(dot_nn(context[0], full_output))]
    attended = [reduce_far(partial[0])]
    contract_other = swap(after(contract_weight, expand_other), half_bit)
    expand_other = after(expand_other, context[0])
    expand_parts = doubled(near(expand_weight, expand_other), 0, 0, last, pair_e)
    sent1 = tied(sent[1], context[0])
    pre = ()
    rows.append(after(gather_near(sent1), partial[0], *pre))
    qkv.append(dot_nn(rows[1], full_qkv).astype(BF16))
    pre = ()
    context.append(attention_forward(after(qkv[1], *pre), *segs[1]))
    expand_got = moved(tied(expand_parts, context[1]), last, pair_e)

    pre = ()
    partial.append(reduce_near(dot_nn(after(context[1], *pre), full_output)))
    attended.append(reduce_far(partial[1]))
    attended[0] = ready(attended[0], partial[1])
    first = [norm_forward(homes[0].astype(F32) + attended[0], gains[0], shifts[0])]
    normed = [first[0][0].astype(BF16)]
    sent = [gather_far(normed[0])]
    contract_other = after(contract_other, context[1])
    pre = (normed[0],)
    first.append(
        norm_forward(homes[1].astype(F32) + ready(attended[1], *pre), gains[0], shifts[0])
    )
    normed.append(first[1][0].astype(BF16))
    sent.append(gather_far(normed[1]))
    cotangent_own, cotangent_send = parted(cotangent)
    contract_parts = near(contract_weight, contract_other)
    expand_got = tied(expand_got, normed[1])
    full_expand = jnp.concatenate(
        [expand_parts[0], expand_got[0], expand_parts[1], expand_got[1]], axis=0
    )
    contract_parts = doubled(tied(contract_parts, *expand_got), 1, 0, last, pair_c)
    normed_rows, active, slope, branch = [], [], [], []
    gate = tuple(contract_parts)
    contract_got = moved(contract_parts, last, pair_c)

    def feed(j, *gate):
        normed_rows.append(after(gather_near(sent[j]), *gate))
        value, derivative = gelu_pair(dot_nn(normed_rows[j], full_expand))
        active.append(value.astype(BF16))
        slope.append(derivative.astype(BF16))

    feed(0, normed[1], *gate)
    cotangent_other = swap(after(cotangent_send, contract_other, active[0]), half_bit)
    feed(1, active[0])
    contract_got = tied(contract_got, active[1])
    full_contract = jnp.concatenate(
        [contract_parts[0], contract_got[0], contract_parts[1], contract_got[1]], axis=1
    )
    gate = active[1]
    branch.append(dot_nn(after(active[0], gate), full_contract).astype(BF16))
    partial = [reduce_near(branch[0])]
    pairs = [reduce_far(partial[0])]
    grads_home, grads_all = to_home(cotangent_own, cotangent_other)
    gate = (branch[0],)
    branch.append(dot_nn(after(active[1], *gate), full_contract).astype(BF16))
    partial.append(reduce_near(branch[1]))
    pairs.append(reduce_far(partial[1]))

    second, branch_grad, sent = [], [], []
    gate = (branch[1], grads_all)
    for j in streams:
        second.append(norm_forward(first[j][0] + ready(pairs[j], *gate), gains[1], shifts[1]))
        branch_grad.append(
            norm_backward(grads_home[j].astype(F32), second[j][1], second[j][2], gains[1])
        )
        gate = (branch_grad[j][0].astype(BF16),)
        sent.append(gather_far(gate[0]))
    result_kept, result_got = sent_home([second[j][0].astype(BF16) for j in streams])
    branch_rows, hidden_grad, normed_part = [], [], []
    partial, pairs = [], []
    gate = (*gate, result_kept)
    for j in streams:
        branch_rows.append(after(gather_near(sent[j]), *gate))
        hidden_grad.append(
            (dot_nt(branch_rows[j], full_contract) * slope[j].astype(F32)).astype(BF16)
        )
        normed_part.append(dot_nt(hidden_grad[j], full_expand).astype(BF16))
        partial.append(reduce_near(normed_part[j]))
        pairs.append(reduce_far(partial[j]))
        if j == 0:
            branch_all = gather_near(sent[1])
            gate = partial[0]
            contract_grad = dot_tn(after(active[0], gate), branch_rows[0])
            contract_grad = contract_grad + dot_tn(active[1], branch_all)
            contract_grad = contract_grad.astype(BF16)
            result_got = after(result_got, partial[0])
            gate = (contract_grad,)
            gate = (*gate, result_got)
    contract_kept, contract_got = split_send(jnp.split(contract_grad, 2, axis=1), last, 1, send_c)
    result = home_pair(result_kept, result_got)
    normed_grad = [branch_grad[0][0] + ready(pairs[0], contract_grad)]
    first_grad = [norm_backward(normed_grad[0], first[0][1], first[0][2], gains[0])]
    gate = first_grad[0][0].astype(BF16)
    sent = [gather_far(gate)]
    expand_grad = dot_tn(after(normed_rows[0], gate, normed_part[1]), hidden_grad[0])
    contract_sum = added(contract_kept, tied(contract_got, partial[1]))
    pre = tuple(contract_sum)
    expand_grad = expand_grad + dot_tn(after(normed_rows[1], *pre), hidden_grad[1])
    expand_grad = expand_grad.astype(BF16)
    contract_kept, contract_got = split_send(contract_sum, last - 1, 1, send_c)
    expand_kept = jnp.split(expand_grad, 2, axis=0)
    expand_kept, expand_got = split_send(expand_kept, last, 0, send_e)
    normed_grad.append(branch_grad[1][0] + ready(pairs[1], expand_grad))
    first_grad.append(norm_backward(normed_grad[1], first[1][1], first[1][2], gains[0]))
    gate = first_grad[1][0].astype(BF16)
    sent.append(gather_far(gate))

    terms = jnp.stack(
        [
            sum(first_grad[j][1][0] for j in streams),
            sum(branch_grad[j][1][0] for j in streams),
            sum(first_grad[j][1][1] for j in streams),
            sum(branch_grad[j][1][1] for j in streams),
        ]
    )

    contract_sum = added(contract_kept, tied(contract_got, expand_grad))
    contract_kept, contract_got = reduce_rest(contract_sum, 1, last - 2)
    pre = (gate, contract_kept)
    attended_rows = [after(gather_near(sent[0]), expand_grad, *pre)]
    context_grad = dot_nt(attended_rows[0], full_output).astype(BF16)
    qkv_grad = [attention_backward(qkv[0], context_grad, *segs[0])]
    attended_rows.append(gather_near(tied(sent[1], qkv_grad[0])))
    expand_sum = added(expand_kept, tied(expand_got, qkv_grad[0]))
    expand_kept, expand_got = split_send(expand_sum, last - 1, 0, send_e)
    pre = tuple(expand_sum)
    tied_grad = after(qkv_grad[0], attended_rows[1], *pre)
    token_part = dot_nt(tied_grad, full_qkv).astype(BF16)
    partial = [reduce_near(token_part)]
    pairs = [reduce_far(partial[0])]
    terms = after(terms, attended_rows[1])
    for bit in t_bits + [core_bit]:
        terms = terms + swap(terms, bit)
    terms = jnp.pad(terms, ((0, extra - 4), (0, 0)))
    pre = ()
    output_grad = dot_tn(after(context[0], partial[0], *pre), attended_rows[0])
    output_grad = output_grad + dot_tn(context[1], attended_rows[1])
    output_grad = jnp.concatenate([output_grad, terms], axis=0).astype(BF16)
    output_kept, output_got = split_send(jnp.split(output_grad, 2, axis=1), last, 1, send_o)
    pre = ()
    context_grad = dot_nt(after(attended_rows[1], output_grad, *pre), full_output)
    qkv_grad.append(attention_backward(qkv[1], context_grad.astype(BF16), *segs[1]))
    expand_kept, expand_got = reduce_rest(
        added(expand_kept, tied(expand_got, qkv_grad[1])), 0, last - 2
    )
    output_sum = added(output_kept, tied(output_got, qkv_grad[1]))
    output_kept, output_got = split_send(output_sum, last - 1, 1, send_o)
    token_sums = [(first_grad[0][0] + ready(pairs[0], qkv_grad[1])).astype(BF16)]
    contract_got = after(contract_got, qkv_grad[1])
    pre = (contract_got,)
    pre = (*pre, token_sums[0])
    pre = (*pre, *output_sum)
    tied_grad = after(qkv_grad[1], expand_kept, *pre)
    token_part = dot_nt(tied_grad, full_qkv).astype(BF16)
    partial.append(reduce_near(token_part))
    pairs.append(reduce_far(partial[1]))
    middle = width // 2
    parts = []
    gate = (partial[1],)
    for i in range(2):
        columns = slice(i * middle, (i + 1) * middle)
        part = dot_tn(after(rows[0][:, columns], *gate), qkv_grad[0])
        parts.append((part + dot_tn(rows[1][:, columns], qkv_grad[1])).astype(BF16))
        if i == 0:
            gate = (parts[0],)
    expand_got = after(expand_got, parts[1])
    pre = (parts[1], expand_got)
    token_sums.append((first_grad[1][0] + ready(pairs[1], *pre)).astype(BF16))
    tokens_kept, tokens_got = sent_home(token_sums)
    output_kept, output_got = reduce_rest(added(output_kept, output_got), 1, last - 2)
    output_got = after(output_got, token_sums[1])
    output_grad = total_of(output_kept, output_got)
    tokens_grad = home_pair(tokens_kept, tokens_got).astype(F32)
    projection_grad = total_of(*reduce_rest(parts, 0, last))
    contract_grad = total_of(contract_kept, contract_got)
    expand_grad = total_of(expand_kept, expand_got)
    projection_grad = projection_grad.reshape(-1, heads, 3, DH)
    query_grad, key_grad, value_grad = [
        projection_grad[:, :, i].reshape(-1, local_width) for i in range(3)
    ]

    return (
        result,
        tokens_grad,
        query_grad,
        key_grad,
        value_grad,
        output_grad[:local_width],
        expand_grad,
        contract_grad,
        output_grad[local_width : local_width + 2],
        output_grad[local_width + 2 : local_width + 4],
    )


def solution(mesh):
    in_specs = (
        P(None, ("dp", "tensor"), None),
        P(None, "dp", None),
        P("dp", "tensor"),
        P("dp", "tensor"),
        P("dp", "tensor"),
        P("tensor", "dp"),
        P("dp", "tensor"),
        P("tensor", "dp"),
        P(None, "dp"),
        P(None, "dp"),
        P(None, ("dp", "tensor"), None),
    )
    out_specs = (
        P(None, ("dp", "tensor"), None),
        P(None, ("dp", "tensor"), None),
        P("dp", "tensor"),
        P("dp", "tensor"),
        P("dp", "tensor"),
        P("tensor", "dp"),
        P("dp", "tensor"),
        P("tensor", "dp"),
        P(None, "dp"),
        P(None, "dp"),
    )
    return jax.shard_map(
        per_device, mesh=mesh, in_specs=in_specs, out_specs=out_specs, check_vma=False
    )
```
